32 devices in a mesh: mem: 8 (over y, x, core), lat: 4 (over z).
Axes of the slice: x: 2, y: 2, z: 4, core: 2. Of those that a mesh axis runs over, the one named last changes fastest.
Arguments:
- coarse_weights: bfloat16 [32, 32, 8, 128], P('lat', 'mem'), may hold values from -6 to 6
- perturbations: bfloat16 [32, 8, 128, 512], P('mem', None, 'lat'), may hold values from -6 to 6
- lat_matrix: bfloat16 [128, 32], P('lat'), may hold values from -1 to 1
- lon_matrix: bfloat16 [128, 512], replicated, may hold values from -0.5 to 0.5
- wind_field: float32 [2, 128, 512], P(None, 'lat', 'mem'), may hold values from -0.4 to 0.4
- observed_cell: int32 [4, 8, 128, 64], P(None, None, 'lat', 'mem'), may hold values from 0 to 7
- observed_value: float32 [4, 8, 128, 64], P(None, None, 'lat', 'mem'), may hold values from -6 to 6
- observed_weight: float32 [4, 8, 128, 64], P(None, None, 'lat', 'mem'), may hold values from 0.5 to 4
Outputs:
- gradient: float32 [32, 32, 8, 128], P('lat', 'mem')
- increment: float32 [8, 128, 512], P(None, 'lat', 'mem')
The draws below stay inside these ranges and needn't reach their ends.
Inputs may be any that keep to these rules, and one draw needn't show every extreme that they name: `observed_cell`: the observed cell is an offset within its block of 8 longitudes.
All inputs are finite; a program needn't handle non-finite values.
Results may differ from the reference program's by a relative error of at most 0.0003.
Values may be sent and summed in bfloat16 or wider, within the bound.
A program may use at most 64 MiB of HBM per device.

```python
import math
import jax
import jax.numpy as jnp
from jax import lax

LEV = 8
STEPS = 4
OBLK = 8
MEMBERS = 32
FLAT = 128
FLON = 512
CLAT = 32
CLON = 128


def touch_ends(result, key, smallest, high):
    longest = result.shape.index(max(result.shape))
    spots = []
    for shift in (0, 1):
        where = [jax.random.randint(jax.random.fold_in(key, axis), (), 0, length) for axis, length in enumerate(result.shape)]
        where[longest] = (where[longest] + shift) % result.shape[longest]
        spots.append(tuple(where))
    return result.at[spots[0]].set(smallest).at[spots[1]].set(high)


def block_scale(own_key, shape, pieces, least, largest):
    level = 1.0
    for axis_at, shards_of in pieces:
        steps = jax.random.uniform(jax.random.fold_in(jax.random.fold_in(own_key, 6), axis_at), (shards_of,), jnp.float32, least / len(pieces), largest / len(pieces))
        level = level * jnp.repeat(jnp.exp(steps), shape[axis_at] // shards_of).reshape((-1,) + (1,) * (len(shape) - 1 - axis_at))
    return level


def centred(own_key, dims, width, limit, pieces=(), kind=jnp.bfloat16):
    drawn = width * jax.random.normal(own_key, dims, jnp.float32)
    if pieces:
        drawn = drawn * block_scale(own_key, dims, pieces, -0.22, 0.18)
    return jnp.clip(drawn, -limit, limit).astype(kind)


def setup_inputs(seed: int = 0) -> dict:
    arg_keys = jax.random.split(jax.random.key(seed), 9)
    coarse_weights = centred(arg_keys[0], (CLAT, MEMBERS, LEV, CLON), 1.0, 6.0, ((0, 4), (1, 8)))
    perturbations = centred(arg_keys[1], (MEMBERS, LEV, FLAT, FLON), 1.0, 6.0, ((0, 8), (2, 4)))
    lat_matrix = centred(arg_keys[2], (FLAT, CLAT), CLAT ** -0.5, 1.0, ((0, 4),))
    lon_matrix = centred(arg_keys[3], (CLON, FLON), CLON ** -0.5, 0.5)
    wind_field = jnp.clip(jax.random.uniform(arg_keys[4], (2, FLAT, FLON), jnp.float32, -0.4, 0.4) * block_scale(arg_keys[4], (2, FLAT, FLON), ((1, 4), (2, 8)), -0.4, 0.0), -0.4, 0.4)
    observed_cell = touch_ends(jax.random.randint(arg_keys[5], (STEPS, LEV, FLAT, FLON // OBLK), 0, OBLK), jax.random.fold_in(arg_keys[5], 1), 0, OBLK - 1).astype(jnp.int32)
    observed_value = centred(arg_keys[6], (STEPS, LEV, FLAT, FLON // OBLK), 1.0, 6.0, ((2, 4), (3, 8)), jnp.float32)
    observed_weight = jnp.clip(jnp.exp(math.log(4.0) - 2.0794415 * jax.random.uniform(arg_keys[7], (STEPS, LEV, FLAT, FLON // OBLK), jnp.float32) ** block_scale(arg_keys[7], (STEPS, LEV, FLAT, FLON // OBLK), ((2, 4), (3, 8)), -0.2, 0.2)), 0.5, 4.0)
    return dict(coarse_weights=coarse_weights, perturbations=perturbations, lat_matrix=lat_matrix, lon_matrix=lon_matrix, wind_field=wind_field, observed_cell=observed_cell, observed_value=observed_value, observed_weight=observed_weight)


diffusion = 0.2
highest = lax.Precision.HIGHEST

def stencil_parts(padded):
    center = padded[:, 1:-1, 1:-1]
    north_cell = padded[:, 2:, 1:-1]
    south_cell = padded[:, :-2, 1:-1]
    east_cell = padded[:, 1:-1, 2:]
    west_cell = padded[:, 1:-1, :-2]
    return (center, north_cell, south_cell, east_cell, west_cell)

def advance(padded, wind_out):
    center, north_cell, south_cell, east_cell, west_cell = stencil_parts(padded)
    spread = north_cell + south_cell + east_cell + west_cell - 4.0 * center
    return center + diffusion * spread - 0.5 * wind_out[1] * (north_cell - south_cell) - 0.5 * wind_out[0] * (east_cell - west_cell)

def retreat(padded, wind_in):
    center, north_cell, south_cell, east_cell, west_cell = stencil_parts(padded)
    spread = north_cell + south_cell + east_cell + west_cell - 4.0 * center
    along_lon = wind_in[0] * padded
    along_lat = wind_in[1] * padded
    return center + diffusion * spread + 0.5 * (along_lat[:, 2:, 1:-1] - along_lat[:, :-2, 1:-1]) + 0.5 * (along_lon[:, 1:-1, 2:] - along_lon[:, 1:-1, :-2])

def observe(tangent, picked, observed, weighting):
    levels, row_count, col_count = tangent.shape
    blocks = tangent.reshape(levels, row_count, col_count // OBLK, OBLK)
    onehot = (picked[..., None] == jnp.arange(OBLK, dtype=jnp.int32)).astype(jnp.float32)
    looked = lax.optimization_barrier(jnp.sum(blocks * onehot, axis=-1))
    misfit = weighting * (looked - observed)
    return (misfit[..., None] * onehot).reshape(levels, row_count, col_count)

def reference(coarse_weights, perturbations, lat_matrix, lon_matrix, wind_field, observed_cell, observed_value, observed_weight):
    member_scale = 1.0 / jnp.sqrt(jnp.float32(MEMBERS - 1))
    lat_full = lat_matrix.astype(jnp.float32)
    lon_full = lon_matrix.astype(jnp.float32)
    by_member = jnp.transpose(coarse_weights, (1, 0, 2, 3))

    def member_term(running, inputs):
        coarse, member = inputs
        partly = jnp.einsum('rc,clw->lrw', lat_full, coarse.astype(jnp.float32), precision=highest)
        localized = jnp.einsum('lrw,wf->lrf', partly, lon_full, precision=highest)
        return (running + localized * member.astype(jnp.float32), None)
    summed, _ = lax.scan(member_term, jnp.zeros((LEV, FLAT, FLON), jnp.float32), (by_member, perturbations))
    increment = summed * member_scale
    margin_one = ((0, 0), (1, 1), (1, 1))
    wind_padded = jnp.pad(wind_field, margin_one)
    tangent = increment
    forcings = []
    for step_index in range(STEPS):
        tangent = advance(jnp.pad(tangent, margin_one), wind_field)
        forcings.append(observe(tangent, observed_cell[step_index], observed_value[step_index], observed_weight[step_index]))
    adjoint = jnp.zeros_like(increment)
    for step_index in reversed(range(STEPS)):
        adjoint = retreat(jnp.pad(adjoint + forcings[step_index], margin_one), wind_padded)

    def member_grad(unused, inputs):
        coarse, member = inputs
        product = member.astype(jnp.float32) * adjoint
        partly = jnp.einsum('lrf,wf->lrw', product, lon_full, precision=highest)
        gradient = jnp.einsum('rc,lrw->clw', lat_full, partly, precision=highest)
        return (unused, gradient * member_scale + coarse.astype(jnp.float32))
    _, grads = lax.scan(member_grad, jnp.float32(0.0), (by_member, perturbations))
    return (jnp.transpose(grads, (1, 0, 2, 3)), increment)
```

```python
import functools

import jax
import jax.numpy as jnp
from jax import lax
from jax.experimental import pallas as pl
from jax.experimental.pallas import tpu as pltpu
from jax.sharding import PartitionSpec as P

STEPS = 4
OBLK = 8
HALO = 2 * STEPS
LAG = 3
LANES = 128
DIFFUSION = 0.2
F32 = jnp.float32
BF16 = jnp.bfloat16


def split2(x):
    hi = x.astype(BF16)
    return hi, (x - hi.astype(F32)).astype(BF16)


def dot(a, b, dims=((1,), (0,))):
    return lax.dot_general(a, b, (dims, ((), ())), preferred_element_type=F32)


def kernel(
    nmem,
    nlat,
    scale,
    coarse_hbm,
    pert_hbm,
    lat_hbm,
    lon_hbm,
    wind_hbm,
    cell_hbm,
    value_hbm,
    weight_hbm,
    grad_ref,
    inc_ref,
    coarse_ref,
    pert_ref,
    lat_ref,
    lon_ref,
    wind_ref,
    cell_ref,
    value_ref,
    weight_ref,
    aux_ref,
    cg,
    auxg,
    part,
    pr,
    rs,
    ext,
    spread,
    coef,
    wts,
    vals,
    itile,
    incr,
    adjg,
    gb,
    gr,
    relayed,
    lon_t,
    in_sem,
    cg_ss,
    cg_rs,
    aux_ss,
    aux_rs,
    ah_ss,
    ah_rs,
    pr_ss,
    pr_rs,
    rs_ss,
    rs_rs,
    halo_ss,
    halo_rs,
    inc_ss,
    inc_rs,
    adj_ss,
    adj_rs,
    rel_ss,
    rel_rs,
    g_ss,
    g_rs,
    relayed_rs,
):
    members, lev, rows, flon = pert_ref.shape
    clon = lon_ref.shape[0]
    cols = flon // nmem
    groups = nmem // lev
    urows = rows // groups
    erows = urows + 2 * HALO
    npairs = nmem // 2
    me = lax.axis_index("mem")
    z = lax.axis_index("lat")
    pair = me // 2
    core = me % 2
    partner = pair * 2 + (1 - core)
    my_level = me // groups
    my_group = me % groups
    my_row = my_group * urows
    block = z * groups + my_group
    has_up = block > 0
    has_down = block < nlat * groups - 1

    def neighbour(shift):
        there = block + shift
        return (my_level * groups + (there + groups) % groups, (there + groups) // groups - 1)

    up = neighbour(-1)
    down = neighbour(1)

    def send(src, dst, ss, rsem, mem, lat):
        return pltpu.make_async_remote_copy(
            src_ref=src,
            dst_ref=dst,
            send_sem=ss,
            recv_sem=rsem,
            device_id={"mem": mem, "lat": lat},
            device_id_type=pl.DeviceIdType.MESH,
        )

    arguments = (
        (coarse_hbm, coarse_ref),
        (lat_hbm, lat_ref),
        (lon_hbm, lon_ref),
        (wind_hbm, wind_ref),
        (cell_hbm, cell_ref),
        (value_hbm, value_ref),
        (weight_hbm, weight_ref),
        (pert_hbm, pert_ref),
    )
    loads = [
        pltpu.make_async_copy(src, dst, in_sem.at[i]) for i, (src, dst) in enumerate(arguments)
    ]
    for load in loads:
        load.start()

    barrier = pltpu.get_barrier_semaphore()

    def greet(mem, lat):
        pl.semaphore_signal(
            barrier, inc=1, device_id={"mem": mem, "lat": lat}, device_id_type=pl.DeviceIdType.MESH
        )

    for i in range(1, nlat):
        greet(me, (z + i) % nlat)
    for i in range(1, nmem):
        greet((me + i) % nmem, z)
    loads[0].wait()
    for m in range(members):
        mine = jnp.swapaxes(coarse_ref[:, m].astype(F32), 0, 1).astype(BF16)
        for level in range(lev):
            cg[z, level, m] = mine[level]
    pl.semaphore_wait(barrier, nmem + nlat - 2)
    if groups > 1:
        far_up = has_up & (my_group == 0)
        far_down = has_down & (my_group == groups - 1)

        @pl.when(far_up)
        def _():
            greet(*up)

        @pl.when(far_down)
        def _():
            greet(*down)

        @pl.when(far_up)
        def _():
            pl.semaphore_wait(barrier, 1)

        @pl.when(far_down)
        def _():
            pl.semaphore_wait(barrier, 1)

    def level_at(i):
        if groups > 1:
            return i
        half = lev // 2
        p = (pair + 1 + i) % npairs
        return 2 * p + jnp.where(i < half, 1 - core, core)

    def cg_copy(there, level):
        return send(
            cg.at[z, level], cg.at[z, level], cg_ss.at[0], cg_rs.at[level], me, there
        )

    def cg_arrivals(level):
        block = cg.at[pl.ds(0, nlat - 1), level]
        return pltpu.make_async_copy(block, block, cg_rs.at[level])

    def spread_coarse(i, carry):
        for j in range(1, nlat):
            cg_copy((z + j) % nlat, level_at(i)).start()
        return carry

    lax.fori_loop(0, lev, spread_coarse, 0)

    for load in loads[1:-1]:
        load.wait()

    blank = jnp.zeros((LANES - 3 * STEPS * (cols // OBLK), rows), F32)
    winds = jnp.concatenate([wind_ref[0], wind_ref[1]], axis=1)

    def pack(level, carry):
        pieces = [ref[t, level] for ref in (weight_ref, value_ref) for t in range(STEPS)]
        pieces += [cell_ref[t, level].astype(F32) for t in range(STEPS)]
        aux_ref[level, :, :LANES] = jnp.transpose(jnp.concatenate(pieces + [blank], axis=0))
        aux_ref[level, :, LANES:] = winds
        return carry

    lax.fori_loop(0, lev, pack, 0)

    def aux_copy(there):
        return send(
            aux_ref.at[there // groups, pl.ds(pl.multiple_of((there % groups) * urows, 8), urows)],
            auxg.at[me, pl.ds(HALO, urows)],
            aux_ss.at[0],
            aux_rs.at[0],
            there,
            z,
        )

    def aux_all(sem):
        block = auxg.at[pl.ds(0, nmem - 1), pl.ds(HALO, urows)]
        return pltpu.make_async_copy(block, block, sem.at[0])

    for i in range(1, nmem):
        aux_copy((me + i) % nmem).start()

    auxg[me, HALO : HALO + urows] = aux_ref[my_level, pl.ds(pl.multiple_of(my_row, 8), urows)]

    @pl.when(jnp.logical_not(has_up))
    def _():
        auxg[:, :HALO] = jnp.zeros((nmem, HALO, 2 * LANES), F32)
        ext[:HALO] = jnp.zeros((HALO, flon), F32)

    @pl.when(jnp.logical_not(has_down))
    def _():
        auxg[:, HALO + urows :] = jnp.zeros((nmem, HALO, 2 * LANES), F32)
        ext[HALO + urows :] = jnp.zeros((HALO, flon), F32)

    per_tile = cols // OBLK
    k = lax.broadcasted_iota(jnp.int32, (2 * LANES, LANES), 0)
    n = lax.broadcasted_iota(jnp.int32, (2 * LANES, LANES), 1)
    for piece in range(3 * STEPS):
        hit = k == (n // cols) * LANES + piece * per_tile + (n % cols) // OBLK
        spread[:, piece * LANES : (piece + 1) * LANES] = jnp.where(hit, 1.0, 0.0).astype(BF16)

    lat_f32 = lat_ref[...].astype(F32)
    lat_bf = lat_ref[...]
    lat_t = jnp.transpose(lat_f32).astype(BF16)
    lat_t2 = jnp.concatenate([lat_t, lat_t], axis=1)
    lon = lon_ref[...]
    lon_t[...] = jnp.transpose(lon.astype(F32)).astype(BF16)

    loads[-1].wait()

    def pr_copy(p):
        unit = 2 * p + (1 - core)
        return send(part.at[unit], pr.at[p], pr_ss.at[0], pr_rs.at[p], partner, z)

    def pr_arrival(p):
        return send(part.at[2 * p + core], pr.at[p], pr_ss.at[0], pr_rs.at[p], partner, z)

    def rs_copy(p):
        return send(pr.at[p], rs.at[pair], rs_ss.at[0], rs_rs.at[0], 2 * p + core, z)

    def rs_all(sem):
        block = rs.at[pl.ds(0, npairs - 1)]
        return pltpu.make_async_copy(block, block, sem.at[0])

    def combine(i, carry):
        p = (pair + 1 + i) % npairs
        pr_arrival(p).wait_recv()
        pr[p] = pr[p] + part[2 * p + core]

        @pl.when(p != pair)
        def _():
            rs_copy(p).start()

        return carry

    ah_up = send(
        auxg.at[:, pl.ds(HALO, HALO)],
        auxg.at[:, pl.ds(HALO + urows, HALO)],
        ah_ss.at[0],
        ah_rs.at[0],
        *up,
    )
    ah_down = send(
        auxg.at[:, pl.ds(urows, HALO)], auxg.at[:, pl.ds(0, HALO)], ah_ss.at[1], ah_rs.at[1], *down
    )


    def exchange_aux():
        aux_all(aux_rs).wait()

        @pl.when(has_up)
        def _():
            ah_up.start()

        @pl.when(has_down)
        def _():
            ah_down.start()

    def forward(i, carry):
        level = level_at(i)
        cg_arrivals(level).wait()
        coarse = jnp.concatenate(
            [cg[:, level, m].astype(F32).reshape(-1, clon) for m in range(members)], axis=1
        ).astype(BF16)
        partly = dot(lat_bf, coarse)
        partly = jnp.concatenate(
            [partly[:, m * clon : (m + 1) * clon] for m in range(members)], axis=0
        )
        hi, lo = split2(partly)
        localized = dot(jnp.concatenate([hi, lo], axis=0), lon)
        localized = localized[: members * rows] + localized[members * rows :]
        total = localized[:rows] * pert_ref[0, level].astype(F32)
        for m in range(1, members):
            total += localized[m * rows : (m + 1) * rows] * pert_ref[m, level].astype(F32)
        part[pl.ds(level * groups, groups)] = total.reshape(groups, urows, flon)

        @pl.when(i == lev // 2)
        def _():
            exchange_aux()

        if groups == 1:

            @pl.when(i < lev // 2)
            def _():
                pr_copy((pair + 1 + i) % npairs).start()

            @pl.when(i >= lev // 2)
            def _():
                combine(i - lev // 2, 0)

        else:
            for g in range(groups // 2):
                pr_copy(level * (groups // 2) + g).start()
        return carry

    lax.fori_loop(0, lev, forward, 0)

    if groups > 1:
        lax.fori_loop(0, npairs, combine, 0)

    @pl.when(has_down)
    def _():
        ah_up_arrival = send(
            auxg.at[:, pl.ds(HALO, HALO)],
            auxg.at[:, pl.ds(HALO + urows, HALO)],
            ah_ss.at[0],
            ah_rs.at[0],
            *down,
        )
        ah_up_arrival.wait_recv()

    @pl.when(has_up)
    def _():
        ah_down_arrival = send(
            auxg.at[:, pl.ds(urows, HALO)],
            auxg.at[:, pl.ds(0, HALO)],
            ah_ss.at[1],
            ah_rs.at[1],
            *up,
        )
        ah_down_arrival.wait_recv()

    @pl.when(has_up)
    def _():
        ah_up.wait_send()

    @pl.when(has_down)
    def _():
        ah_down.wait_send()

    place = block * urows - HALO + lax.broadcasted_iota(jnp.int32, (erows, LANES), 0)
    inside = (place >= 0) & (place < nlat * rows)
    lane = lax.broadcasted_iota(jnp.int32, (erows, LANES), 1)
    tiles = LANES // cols
    for q in range(flon // LANES):
        first, second = auxg[tiles * q], auxg[tiles * q + 1]
        lhs = jnp.concatenate([first[:, :LANES], second[:, :LANES]], axis=1)
        hi, rest = lhs.astype(BF16), lhs
        rest = rest - hi.astype(F32)
        mid, low = split2(rest)
        out = dot(jnp.concatenate([hi, mid, low], axis=0), spread[...])
        out = out[:erows] + out[erows : 2 * erows] + out[2 * erows :]
        at = slice(q * LANES, (q + 1) * LANES)
        for t in range(STEPS):
            weight = out[:, t * LANES : (t + 1) * LANES]
            value = out[:, (STEPS + t) * LANES : (STEPS + t + 1) * LANES]
            cell = out[:, (2 * STEPS + t) * LANES : (2 * STEPS + t + 1) * LANES]
            hit = cell == (lane % OBLK).astype(F32)
            wts[t, :, at] = jnp.where(hit, weight, 0.0)
            vals[t, :, at] = value
        w0, w1 = first[:, LANES:], second[:, LANES:]
        lower = lane < cols
        c0 = jnp.where(lower, w0, pltpu.roll(w1, cols, 1))
        c1 = jnp.where(lower, pltpu.roll(w0, cols, 1), w1)
        east_in = inside & (lane + q * LANES < flon - 1)
        west_in = inside & (lane + q * LANES > 0)
        coef[0, :, at] = jnp.where(inside, DIFFUSION - 0.5 * c1, 0.0)
        coef[1, :, at] = jnp.where(inside, DIFFUSION + 0.5 * c1, 0.0)
        coef[2, :, at] = jnp.where(east_in, DIFFUSION - 0.5 * c0, 0.0)
        coef[3, :, at] = jnp.where(west_in, DIFFUSION + 0.5 * c0, 0.0)
        coef[4, :, at] = jnp.where(inside, jnp.full((erows, LANES), 1.0 - 4.0 * DIFFUSION, F32), 0.0)

    total = pr[pair]
    rs_all(rs_rs).wait()
    for i in range(1, npairs):
        p = (pair + npairs - i) % npairs
        total = total + rs[p]
    total = total * scale
    ext[HALO : HALO + urows] = total
    halo_up = send(
        ext.at[pl.ds(HALO, HALO)],
        ext.at[pl.ds(HALO + urows, HALO)],
        halo_ss.at[0],
        halo_rs.at[0],
        *up,
    )
    halo_down = send(
        ext.at[pl.ds(urows, HALO)], ext.at[pl.ds(0, HALO)], halo_ss.at[1], halo_rs.at[1], *down
    )

    @pl.when(has_up)
    def _():
        halo_up.start()

    @pl.when(has_down)
    def _():
        halo_down.start()

    for m in range(nmem):
        itile[m] = total[:, m * cols : (m + 1) * cols]

    def inc_copy(there):
        return send(
            itile.at[there],
            incr.at[my_level, pl.ds(pl.multiple_of(my_row, 8), urows)],
            inc_ss.at[0],
            inc_rs.at[0],
            there,
            z,
        )

    def inc_all(sem):
        block = itile.at[pl.ds(0, nmem - 1)]
        return pltpu.make_async_copy(block, block, sem.at[0])

    for i in range(1, nmem):
        inc_copy((me + i) % nmem).start()
    incr[my_level, pl.ds(pl.multiple_of(my_row, 8), urows)] = itile[me]

    @pl.when(has_down)
    def _():
        send(
            ext.at[pl.ds(HALO, HALO)],
            ext.at[pl.ds(HALO + urows, HALO)],
            halo_ss.at[0],
            halo_rs.at[0],
            *down,
        ).wait_recv()

    @pl.when(has_up)
    def _():
        send(
            ext.at[pl.ds(urows, HALO)], ext.at[pl.ds(0, HALO)], halo_ss.at[1], halo_rs.at[1], *up
        ).wait_recv()

    @pl.when(has_up)
    def _():
        halo_up.wait_send()

    @pl.when(has_down)
    def _():
        halo_down.wait_send()

    state = ext[...]
    forcing = []
    for t in range(STEPS):
        state = (
            coef[4] * state
            + coef[0] * pltpu.roll(state, erows - 1, 0)
            + coef[1] * pltpu.roll(state, 1, 0)
            + coef[2] * pltpu.roll(state, flon - 1, 1)
            + coef[3] * pltpu.roll(state, 1, 1)
        )
        wts[t] = wts[t] * (state - vals[t])
    adjoint = None
    for t in reversed(range(STEPS)):
        adjoint = wts[t] if adjoint is None else adjoint + wts[t]
        adjoint = (
            coef[4] * adjoint
            + pltpu.roll(coef[1] * adjoint, erows - 1, 0)
            + pltpu.roll(coef[0] * adjoint, 1, 0)
            + pltpu.roll(coef[3] * adjoint, flon - 1, 1)
            + pltpu.roll(coef[2] * adjoint, 1, 1)
        )
    adjg[me] = adjoint[HALO : HALO + urows]

    def adj_copy(p):
        return send(adjg.at[me], adjg.at[me], adj_ss.at[0], adj_rs.at[pair], 2 * p + core, z)

    def adj_arrival(p):
        unit = 2 * p + core
        return send(adjg.at[unit], adjg.at[unit], adj_ss.at[0], adj_rs.at[p], unit, z)

    def relay(p):
        unit = 2 * p + core
        return send(adjg.at[unit], adjg.at[unit], rel_ss.at[0], rel_rs.at[p], partner, z)

    def relay_arrival(p):
        unit = 2 * p + (1 - core)
        return send(adjg.at[unit], adjg.at[unit], rel_ss.at[0], rel_rs.at[p], partner, z)

    for i in range(1, npairs):
        adj_copy((pair + i) % npairs).start()

    directions = ((0, 1), (1, -1))

    def g_target(way, step, k, there, level):
        if k >= 3:
            return z + step, relayed.at[way, k - 3, level], relayed_rs.at[way, k - 3, level]
        slot = 2 * way + k - 1
        return there, gr.at[slot, level], g_rs.at[slot]

    def g_copy(way, step, k, level):
        there = z + step * k
        lat, dst, arrived = g_target(way, step, k, there, level)
        return send(gb.at[there, level], dst, g_ss.at[0], arrived, me, lat)

    def exists(place):
        return (place >= 0) & (place < nlat)

    def g_first(level):
        for k in range(nlat - 1, 0, -1):
            for way, step in directions:
                ready = exists(z + step * k)
                if k > 1:
                    ready = ready & jnp.logical_not(exists(z - step))

                @pl.when(ready)
                def _():
                    g_copy(way, step, k, level).start()

    def g_later(level):
        for k in range(nlat - 2, 1, -1):
            for way, step in directions:
                there = z + step * k

                @pl.when(exists(there) & exists(z - step))
                def _():
                    send(
                        gb.at[there, level],
                        relayed.at[way, k - 2, level],
                        g_ss.at[0],
                        relayed_rs.at[way, k - 2, level],
                        me,
                        z - step,
                    ).wait_recv()
                    gb[there, level] = gb[there, level] + relayed[way, k - 2, level]
                    g_copy(way, step, k, level).start()

    def backward(level):
        field = adjg[pl.ds(level * groups, groups)].reshape(rows, flon)
        product = jnp.concatenate(
            [pert_ref[m, level].astype(F32) * field for m in range(members)], axis=0
        )
        hi, lo = split2(product)
        projected = dot(jnp.concatenate([hi, lo], axis=0), lon_t[...])
        projected = projected[: members * rows] + projected[members * rows :]
        projected = jnp.concatenate(
            [projected[m * rows : (m + 1) * rows] for m in range(members)], axis=1
        )
        hi, lo = split2(projected)
        banded = dot(lat_t2, jnp.concatenate([hi, lo], axis=0))
        gb[:, level] = banded.reshape(nlat, -1, members * clon)
        g_first(level)

    def order(j):
        if groups == 2:
            return (pair + npairs - j) % npairs
        near_turn = (j == 0) | ((j >= 2) & (j <= npairs))
        i = jnp.where(j < 2, 0, jnp.where(near_turn, j - 1, j - npairs))
        return 2 * ((pair + npairs - i) % npairs) + jnp.where(near_turn, core, 1 - core)

    def step_back(j):
        backward(order(j))

        @pl.when(j >= LAG)
        def _():
            g_later(order(j - LAG))

    def near(i, carry):
        p = (pair + npairs - i) % npairs

        @pl.when(i > 0)
        def _():
            adj_arrival(p).wait_recv()

        relay(p).start()
        if groups == 1:
            step_back(jnp.where(i == 0, 0, i + 1))
        return carry


    def far(i, carry):
        p = (pair + npairs - i) % npairs
        relay_arrival(p).wait_recv()
        step_back(jnp.where(i == 0, 1, npairs + i) if groups == 1 else i)
        return carry

    for first, last in ((0, 1), (1, npairs)):
        lax.fori_loop(first, last, near, 0)
        lax.fori_loop(first, last, far, 0)

    def trail(j, carry):
        g_later(order(j))
        return carry

    lax.fori_loop(lev - LAG, lev, trail, 0)

    inc_all(inc_rs).wait()
    inc_ref[...] = incr[...].reshape(lev * rows, cols)

    for k in range(1, min(3, nlat)):
        for way, step in directions:
            source = z - step * k
            slot = 2 * way + k - 1

            @pl.when(exists(source))
            def _():
                pltpu.make_async_copy(gr.at[slot], gr.at[slot], g_rs.at[slot]).wait()
                gb[z] = gb[z] + gr[slot]

    for m in range(members):
        total = jnp.swapaxes(gb[z, :, :, m * clon : (m + 1) * clon], 0, 1)
        total = total * scale
        for c in range(total.shape[0]):
            at = (c * members + m) * lev
            grad_ref[at : at + lev] = total[c] + coarse_ref[c, m].astype(F32)

    aux_all(aux_ss).wait()
    inc_all(inc_ss).wait()
    rs_all(rs_ss).wait()

    def sent(block, sem):
        pltpu.make_async_copy(block, block, sem.at[0]).wait()

    sent(pr, pr_ss)
    sent(adjg.at[pl.ds(0, npairs)], rel_ss)
    sent(adjg.at[pl.ds(0, npairs - 1)], adj_ss)
    sent(cg.at[pl.ds(0, nlat - 1)], cg_ss)
    sent(gb.at[pl.ds(0, nlat - 1)], g_ss)


def finish_kernel(banded_ref, tiles_ref, grad_ref, inc_ref):
    grad_ref[...] = banded_ref[...]
    inc_ref[...] = tiles_ref[...]


def body(
    nmem,
    nlat,
    coarse_weights,
    perturbations,
    lat_matrix,
    lon_matrix,
    wind_field,
    observed_cell,
    observed_value,
    observed_weight,
):
    members, lev, rows, flon = perturbations.shape
    cband, _, _, clon = coarse_weights.shape
    cols = wind_field.shape[2]
    blocks = cols // OBLK
    groups = nmem // lev
    urows = rows // groups
    erows = urows + 2 * HALO
    npairs = nmem // 2
    assert nmem == lev * groups and nmem % 2 == 0 and groups <= 2 and urows % 8 == 0 and urows >= HALO
    assert 2 * cols == LANES and 3 * STEPS * blocks <= LANES
    vmem = pl.BlockSpec(memory_space=pltpu.VMEM)
    dma = pltpu.SemaphoreType.DMA
    width = members * clon
    arguments = (
        coarse_weights,
        perturbations,
        lat_matrix,
        lon_matrix,
        wind_field,
        jnp.swapaxes(observed_cell, 2, 3),
        jnp.swapaxes(observed_value, 2, 3),
        jnp.swapaxes(observed_weight, 2, 3),
    )
    banded, increment = pl.pallas_call(
        functools.partial(kernel, nmem, nlat, float(1.0 / (members * nmem - 1) ** 0.5)),
        out_shape=(
            pltpu.VMEM((cband * members * lev, clon), F32),
            pltpu.VMEM((lev * rows, cols), F32),
        ),
        in_specs=[pl.BlockSpec(memory_space=pltpu.HBM)] * len(arguments),
        out_specs=(vmem, vmem),
        scratch_shapes=[
            *[pltpu.VMEM(x.shape, x.dtype) for x in arguments],
            pltpu.VMEM((lev, rows, 2 * LANES), F32),
            pltpu.VMEM((nlat, lev, members, cband, clon), BF16),
            pltpu.VMEM((nmem, erows, 2 * LANES), F32),
            pltpu.VMEM((nmem, urows, flon), F32),
            pltpu.VMEM((npairs, urows, flon), F32),
            pltpu.VMEM((npairs, urows, flon), F32),
            pltpu.VMEM((erows, flon), F32),
            pltpu.VMEM((2 * LANES, 3 * STEPS * LANES), BF16),
            pltpu.VMEM((5, erows, flon), F32),
            pltpu.VMEM((STEPS, erows, flon), F32),
            pltpu.VMEM((STEPS, erows, flon), F32),
            pltpu.VMEM((nmem, urows, cols), F32),
            pltpu.VMEM((lev, rows, cols), F32),
            pltpu.VMEM((nmem, urows, flon), F32),
            pltpu.VMEM((nlat, lev, cband, width), F32),
            pltpu.VMEM((4, lev, cband, width), F32),
            pltpu.VMEM((2, max(1, nlat - 3), lev, cband, width), F32),
            pltpu.VMEM((flon, clon), BF16),
            dma((len(arguments),)),
            dma((1,)),
            dma((lev,)),
            dma((1,)),
            dma((1,)),
            dma((2,)),
            dma((2,)),
            dma((1,)),
            dma((npairs,)),
            dma((1,)),
            dma((1,)),
            dma((2,)),
            dma((2,)),
            dma((1,)),
            dma((1,)),
            dma((1,)),
            dma((npairs,)),
            dma((1,)),
            dma((npairs,)),
            dma((1,)),
            dma((4,)),
            dma((2, max(1, nlat - 3), lev)),
        ],
        compiler_params=pltpu.CompilerParams(
            collective_id=0, has_side_effects=True, vmem_limit_bytes=40 * 1024 * 1024
        ),
    )(*[pltpu.with_memory_space_constraint(x, pltpu.HBM) for x in arguments])
    gradient, increment = pl.pallas_call(
        finish_kernel,
        out_shape=(
            jax.ShapeDtypeStruct((cband * members * lev, clon), F32),
            jax.ShapeDtypeStruct((lev * rows, cols), F32),
        ),
        in_specs=[vmem] * 2,
        out_specs=(vmem, vmem),
        compiler_params=pltpu.CompilerParams(vmem_limit_bytes=4 * 1024 * 1024),
    )(banded, increment)
    return gradient.reshape(coarse_weights.shape), increment.reshape(lev, rows, cols)


def solution(mesh):
    in_specs = (
        P("lat", "mem", None, None),
        P("mem", None, "lat", None),
        P("lat", None),
        P(),
        P(None, "lat", "mem"),
        P(None, None, "lat", "mem"),
        P(None, None, "lat", "mem"),
        P(None, None, "lat", "mem"),
    )
    out_specs = (P("lat", "mem", None, None), P(None, "lat", "mem"))
    call = functools.partial(body, mesh.shape["mem"], mesh.shape["lat"])
    return jax.shard_map(call, mesh=mesh, in_specs=in_specs, out_specs=out_specs, check_vma=False)
```

```python
import functools

import jax
import jax.numpy as jnp
from jax import lax
from jax.experimental import pallas as pl
from jax.experimental.pallas import tpu as pltpu
from jax.sharding import PartitionSpec as P

STEPS = 4
OBLK = 8
HALO = 2 * STEPS
SUB = 8
LAG = 3
LANES = 128
ROW = 4 * LANES
DIFFUSION = 0.2
CODES = 32767.0
TINY = 1e-30
F32 = jnp.float32
BF16 = jnp.bfloat16
I16 = jnp.int16


def split2(x):
    hi = x.astype(BF16)
    return hi, (x - hi.astype(F32)).astype(BF16)


def dot(a, b, dims=((1,), (0,))):
    return lax.dot_general(a, b, (dims, ((), ())), preferred_element_type=F32)


def spans(width):
    return [slice(at, at + LANES) for at in range(0, width, LANES)]


def encode(x):
    size = jnp.abs(x)
    peak = functools.reduce(jnp.maximum, [size[i] for i in range(x.shape[0])])
    peak = functools.reduce(jnp.maximum, [peak[:, at] for at in spans(x.shape[2])])
    step = jnp.maximum(jnp.max(peak, axis=0, keepdims=True), TINY) * (1.0 / CODES)
    inverse = 1.0 / step
    scaled = jnp.concatenate([x[:, :, at] * inverse for at in spans(x.shape[2])], axis=2)
    return jnp.round(scaled).astype(jnp.int32).astype(I16), step


def decode(codes, step):
    values = codes.astype(F32)
    return jnp.concatenate([values[..., at] * step for at in spans(codes.shape[-1])], axis=-1)


def kernel(
    nmem,
    nlat,
    scale,
    coarse_hbm,
    pert_hbm,
    lat_hbm,
    lon_hbm,
    wind_hbm,
    cell_hbm,
    value_hbm,
    weight_hbm,
    grad_ref,
    inc_ref,
    coarse_ref,
    pert_ref,
    lat_ref,
    lon_ref,
    wind_ref,
    cell_ref,
    value_ref,
    weight_ref,
    aux_ref,
    cg,
    auxg,
    part,
    pr,
    rq,
    rq_step,
    rs,
    rs_step,
    hq,
    hq_step,
    ext,
    spread,
    coef,
    wts,
    vals,
    itile,
    incr,
    adjq,
    adj_step,
    gb,
    gq,
    gq_step,
    gr,
    gr_step,
    relayed,
    relayed_step,
    lon_t,
    lon_2,
    amount,
    in_sem,
    cg_ss,
    cg_rs,
    aux_ss,
    aux_rs,
    ah_ss,
    ah_rs,
    pr_ss,
    pr_rs,
    rs_ss,
    rs_rs,
    halo_ss,
    halo_rs,
    inc_ss,
    inc_rs,
    adj_ss,
    adj_rs,
    rel_ss,
    rel_rs,
    g_ss,
    g_rs,
    relayed_rs,
):
    members, lev, rows, flon = pert_ref.shape
    clon = lon_ref.shape[0]
    cband, width = gb.shape[2:]
    cols = flon // nmem
    groups = nmem // lev
    urows = rows // groups
    erows = urows + 2 * HALO
    npairs = nmem // 2
    me = lax.axis_index("mem")
    z = lax.axis_index("lat")
    pair = me // 2
    core = me % 2
    partner = pair * 2 + (1 - core)
    my_level = me // groups
    my_group = me % groups
    my_row = my_group * urows
    block = z * groups + my_group
    has_up = block > 0
    has_down = block < nlat * groups - 1
    unit_bytes = urows * flon * 2 + ROW
    edge_bytes = HALO * flon * 2 + ROW
    band_bytes = cband * width * 2 + ROW

    def neighbour(unit, shift):
        there = block + shift
        home = (unit // groups) * groups
        return home + (there + groups) % groups, (there + groups) // groups - 1

    up = neighbour(me, -1)
    down = neighbour(me, 1)

    def send(src, dst, ss, rsem, mem, lat):
        return pltpu.make_async_remote_copy(
            src_ref=src,
            dst_ref=dst,
            send_sem=ss,
            recv_sem=rsem,
            device_id={"mem": mem, "lat": lat},
            device_id_type=pl.DeviceIdType.MESH,
        )

    def await_bytes(count, sem):
        these = amount.at[pl.ds(0, count // ROW)]
        pltpu.make_async_copy(these, these, sem).wait()

    arguments = (
        (coarse_hbm, coarse_ref),
        (lat_hbm, lat_ref),
        (lon_hbm, lon_ref),
        (wind_hbm, wind_ref),
        (cell_hbm, cell_ref),
        (value_hbm, value_ref),
        (weight_hbm, weight_ref),
        (pert_hbm, pert_ref),
    )
    loads = [
        pltpu.make_async_copy(src, dst, in_sem.at[i]) for i, (src, dst) in enumerate(arguments)
    ]
    for load in loads:
        load.start()

    barrier = pltpu.get_barrier_semaphore()

    def greet(mem, lat):
        pl.semaphore_signal(
            barrier, inc=1, device_id={"mem": mem, "lat": lat}, device_id_type=pl.DeviceIdType.MESH
        )

    for i in range(1, nlat):
        greet(me, (z + i) % nlat)
    for i in range(1, nmem):
        greet((me + i) % nmem, z)
    far_up = has_up & (my_group == 0)
    far_down = has_down & (my_group == groups - 1)
    others = range(1, npairs) if groups == 1 else range(npairs)

    @pl.when(far_up)
    def _():
        for i in others:
            greet(*neighbour(2 * ((pair + i) % npairs) + core, -1))

    @pl.when(far_down)
    def _():
        for i in others:
            greet(*neighbour(2 * ((pair + i) % npairs) + core, 1))

    loads[0].wait()
    for m in range(members):
        mine = jnp.swapaxes(coarse_ref[:, m].astype(F32), 0, 1).astype(BF16)
        for level in range(lev):
            cg[z, level, m] = mine[level]
    more = jnp.where(far_up, len(others), 0) + jnp.where(far_down, len(others), 0)
    pl.semaphore_wait(barrier, nmem + nlat - 2 + more)

    def turn(i):
        last = 2 * npairs - 1
        theirs = (i == 0) | ((i % 2 == 1) & (i < last))
        away = jnp.where(theirs, npairs - 1 - (i + 1) // 2, npairs - i // 2)
        return theirs, pair ^ jnp.where(i == last, 0, away)

    def level_at(i):
        if groups > 1:
            return i
        theirs, p = turn(i)
        return 2 * p + jnp.where(theirs, 1 - core, core)

    def cg_copy(there, level):
        return send(cg.at[z, level], cg.at[z, level], cg_ss.at[0], cg_rs.at[level], me, there)

    def spread_coarse(i, carry):
        for j in range(1, nlat):
            cg_copy((z + j) % nlat, level_at(i)).start()
        return carry

    lax.fori_loop(0, lev, spread_coarse, 0)

    for load in loads[1:-1]:
        load.wait()

    blank = jnp.zeros((LANES - 3 * STEPS * (cols // OBLK), rows), F32)
    winds = jnp.concatenate([wind_ref[0], wind_ref[1]], axis=1)

    def pack(level, carry):
        pieces = [ref[t, level] for ref in (weight_ref, value_ref) for t in range(STEPS)]
        pieces += [cell_ref[t, level].astype(F32) for t in range(STEPS)]
        aux_ref[level, :, :LANES] = jnp.transpose(jnp.concatenate(pieces + [blank], axis=0))
        aux_ref[level, :, LANES:] = winds
        return carry

    lax.fori_loop(0, lev, pack, 0)

    def aux_copy(there):
        return send(
            aux_ref.at[there // groups, pl.ds(pl.multiple_of((there % groups) * urows, 8), urows)],
            auxg.at[me, pl.ds(HALO, urows)],
            aux_ss.at[0],
            aux_rs.at[0],
            there,
            z,
        )

    def aux_all(sem):
        these = auxg.at[pl.ds(0, nmem - 1), pl.ds(HALO, urows)]
        return pltpu.make_async_copy(these, these, sem.at[0])

    for i in range(1, nmem):
        aux_copy((me + i) % nmem).start()

    auxg[me, HALO : HALO + urows] = aux_ref[my_level, pl.ds(pl.multiple_of(my_row, 8), urows)]

    @pl.when(jnp.logical_not(has_up))
    def _():
        auxg[:, :HALO] = jnp.zeros((nmem, HALO, 2 * LANES), F32)
        ext[:HALO] = jnp.zeros((HALO, flon), F32)

    @pl.when(jnp.logical_not(has_down))
    def _():
        auxg[:, HALO + urows :] = jnp.zeros((nmem, HALO, 2 * LANES), F32)
        ext[HALO + urows :] = jnp.zeros((HALO, flon), F32)

    per_tile = cols // OBLK
    k = lax.broadcasted_iota(jnp.int32, (2 * LANES, LANES), 0)
    n = lax.broadcasted_iota(jnp.int32, (2 * LANES, LANES), 1)
    for piece in range(3 * STEPS):
        hit = k == (n // cols) * LANES + piece * per_tile + (n % cols) // OBLK
        spread[:, piece * LANES : (piece + 1) * LANES] = jnp.where(hit, 1.0, 0.0).astype(BF16)

    lat_f32 = lat_ref[...].astype(F32)
    lat_bf = lat_ref[...]
    lat_t = jnp.transpose(lat_f32).astype(BF16)
    lat_t2 = jnp.concatenate([lat_t, lat_t], axis=1)
    lon = lon_ref[...]
    lon_t[...] = jnp.transpose(lon.astype(F32)).astype(BF16)
    lon_2[:clon] = lon
    lon_2[clon:] = lon

    loads[-1].wait()

    def pr_copy(p):
        unit = 2 * p + (1 - core)
        return send(part.at[unit], pr.at[p], pr_ss.at[0], pr_rs.at[p], partner, z)

    def pr_arrival(p):
        return send(part.at[2 * p + core], pr.at[p], pr_ss.at[0], pr_rs.at[p], partner, z)

    def rs_copies(p):
        unit = 2 * p + core
        return (
            send(rq.at[p], rs.at[pair], rs_ss.at[0], rs_rs.at[0], unit, z),
            send(rq_step.at[p], rs_step.at[pair], rs_ss.at[0], rs_rs.at[0], unit, z),
        )

    def halo_copies(p, side):
        mem, lat = neighbour(2 * p + core, 1 if side == 0 else -1)
        rim = urows // SUB - 1 if side == 0 else 0
        sems = halo_ss.at[side], halo_rs.at[side]
        return (
            send(rq.at[p, rim], hq.at[side, pair], *sems, mem, lat),
            send(rq_step.at[p], hq_step.at[side, pair], *sems, mem, lat),
        )

    def combine(p):
        pr_arrival(p).wait_recv()
        whole = pr[p] + part[2 * p + core]
        pr[p] = whole
        rq[p], rq_step[p] = encode(whole.reshape(urows // SUB, SUB, flon))

        @pl.when(p != pair)
        def _():
            for copy in rs_copies(p):
                copy.start()

        @pl.when(has_down)
        def _():
            for copy in halo_copies(p, 0):
                copy.start()

        @pl.when(has_up)
        def _():
            for copy in halo_copies(p, 1):
                copy.start()

    ah_up = send(
        auxg.at[:, pl.ds(HALO, HALO)],
        auxg.at[:, pl.ds(HALO + urows, HALO)],
        ah_ss.at[0],
        ah_rs.at[0],
        *up,
    )
    ah_down = send(
        auxg.at[:, pl.ds(urows, HALO)], auxg.at[:, pl.ds(0, HALO)], ah_ss.at[1], ah_rs.at[1], *down
    )

    def exchange_aux():
        aux_all(aux_rs).wait()

        @pl.when(has_up)
        def _():
            ah_up.start()

        @pl.when(has_down)
        def _():
            ah_down.start()

    def forward(i, carry):
        level = level_at(i)
        arrived = cg.at[pl.ds(0, nlat - 1), level]
        pltpu.make_async_copy(arrived, arrived, cg_rs.at[level]).wait()
        coarse = jnp.concatenate(
            [cg[:, level, m].astype(F32).reshape(-1, clon) for m in range(members)], axis=1
        ).astype(BF16)
        partly = dot(lat_bf, coarse)
        partly = jnp.concatenate(
            [partly[:, m * clon : (m + 1) * clon] for m in range(members)], axis=0
        )
        localized = dot(jnp.concatenate(split2(partly), axis=1), lon_2[...])
        total = localized[:rows] * pert_ref[0, level].astype(F32)
        for m in range(1, members):
            total += localized[m * rows : (m + 1) * rows] * pert_ref[m, level].astype(F32)
        part[pl.ds(level * groups, groups)] = total.reshape(groups, urows, flon)

        @pl.when(i == lev // 2)
        def _():
            exchange_aux()

        if groups == 1:
            theirs, p = turn(i)

            @pl.when(theirs)
            def _():
                pr_copy(p).start()

            @pl.when(jnp.logical_not(theirs))
            def _():
                combine(p)

        else:
            for g in range(groups // 2):
                pr_copy(level * (groups // 2) + g).start()
        return carry

    lax.fori_loop(0, lev, forward, 0)

    if groups > 1:

        def combine_at(i, carry):
            combine(pair ^ (npairs - 1 - i))
            return carry

        lax.fori_loop(0, npairs, combine_at, 0)

    rim = auxg.at[:, pl.ds(0, HALO)]

    @pl.when(has_down)
    def _():
        pltpu.make_async_copy(rim, rim, ah_rs.at[0]).wait()

    @pl.when(has_up)
    def _():
        pltpu.make_async_copy(rim, rim, ah_rs.at[1]).wait()

    place = block * urows - HALO + lax.broadcasted_iota(jnp.int32, (erows, LANES), 0)
    inside = (place >= 0) & (place < nlat * rows)
    lane = lax.broadcasted_iota(jnp.int32, (erows, LANES), 1)
    tiles = LANES // cols
    for q in range(flon // LANES):
        first, second = auxg[tiles * q], auxg[tiles * q + 1]
        lhs = jnp.concatenate([first[:, :LANES], second[:, :LANES]], axis=1)
        hi, rest = lhs.astype(BF16), lhs
        rest = rest - hi.astype(F32)
        mid, low = split2(rest)
        out = dot(jnp.concatenate([hi, mid, low], axis=0), spread[...])
        out = out[:erows] + out[erows : 2 * erows] + out[2 * erows :]
        at = slice(q * LANES, (q + 1) * LANES)
        for t in range(STEPS):
            weight = out[:, t * LANES : (t + 1) * LANES]
            value = out[:, (STEPS + t) * LANES : (STEPS + t + 1) * LANES]
            cell = out[:, (2 * STEPS + t) * LANES : (2 * STEPS + t + 1) * LANES]
            hit = cell == (lane % OBLK).astype(F32)
            wts[t, :, at] = jnp.where(hit, weight, 0.0)
            vals[t, :, at] = value
        w0, w1 = first[:, LANES:], second[:, LANES:]
        lower = lane < cols
        c0 = jnp.where(lower, w0, pltpu.roll(w1, cols, 1))
        c1 = jnp.where(lower, pltpu.roll(w0, cols, 1), w1)
        east_in = inside & (lane + q * LANES < flon - 1)
        west_in = inside & (lane + q * LANES > 0)
        coef[0, :, at] = jnp.where(inside, DIFFUSION - 0.5 * c1, 0.0)
        coef[1, :, at] = jnp.where(inside, DIFFUSION + 0.5 * c1, 0.0)
        coef[2, :, at] = jnp.where(east_in, DIFFUSION - 0.5 * c0, 0.0)
        coef[3, :, at] = jnp.where(west_in, DIFFUSION + 0.5 * c0, 0.0)
        coef[4, :, at] = jnp.where(inside, jnp.full((erows, LANES), 1.0 - 4.0 * DIFFUSION, F32), 0.0)

    await_bytes((npairs - 1) * unit_bytes, rs_rs.at[0])
    total = pr[pair]
    for i in range(1, npairs):
        p = pair ^ i
        total = total + decode(rs[p], rs_step[p]).reshape(urows, flon)
    total = total * scale
    ext[HALO : HALO + urows] = total

    def rim_total(side):
        await_bytes(npairs * edge_bytes, halo_rs.at[side])
        return sum(decode(hq[side, p], hq_step[side, p]) for p in range(npairs)) * scale

    @pl.when(has_up)
    def _():
        ext[:HALO] = rim_total(0)

    @pl.when(has_down)
    def _():
        ext[HALO + urows :] = rim_total(1)

    state = ext[...]
    for t in range(STEPS):
        state = (
            coef[4] * state
            + coef[0] * pltpu.roll(state, erows - 1, 0)
            + coef[1] * pltpu.roll(state, 1, 0)
            + coef[2] * pltpu.roll(state, flon - 1, 1)
            + coef[3] * pltpu.roll(state, 1, 1)
        )
        wts[t] = wts[t] * (state - vals[t])
    adjoint = None
    for t in reversed(range(STEPS)):
        adjoint = wts[t] if adjoint is None else adjoint + wts[t]
        adjoint = (
            coef[4] * adjoint
            + pltpu.roll(coef[1] * adjoint, erows - 1, 0)
            + pltpu.roll(coef[0] * adjoint, 1, 0)
            + pltpu.roll(coef[3] * adjoint, flon - 1, 1)
            + pltpu.roll(coef[2] * adjoint, 1, 1)
        )
    adjq[me], adj_step[me] = encode(
        adjoint[HALO : HALO + urows].reshape(urows // SUB, SUB, flon)
    )

    def unit_copies(unit, ss, rsem, mem):
        return (
            send(adjq.at[unit], adjq.at[unit], ss, rsem, mem, z),
            send(adj_step.at[unit], adj_step.at[unit], ss, rsem, mem, z),
        )

    for i in range(1, npairs):
        for copy in unit_copies(me, adj_ss.at[0], adj_rs.at[pair], 2 * (pair ^ i) + core):
            copy.start()

    def relay(p):
        for copy in unit_copies(2 * p + core, rel_ss.at[0], rel_rs.at[p], partner):
            copy.start()

    def inc_copy(there):
        return send(
            itile.at[there],
            incr.at[my_level, pl.ds(pl.multiple_of(my_row, 8), urows)],
            inc_ss.at[0],
            inc_rs.at[0],
            there,
            z,
        )

    def inc_all(sem):
        these = itile.at[pl.ds(0, nmem - 1)]
        return pltpu.make_async_copy(these, these, sem.at[0])

    def share_increment():
        for m in range(nmem):
            itile[m] = ext[HALO : HALO + urows, m * cols : (m + 1) * cols]
        for i in range(1, nmem):
            inc_copy((me + i) % nmem).start()
        incr[my_level, pl.ds(pl.multiple_of(my_row, 8), urows)] = itile[me]

    directions = ((0, 1), (1, -1))

    def g_copies(way, step, k, level):
        there = z + step * k
        src = gq.at[there, level], gq_step.at[there, level]
        if k >= 3:
            lat, arrived = z + step, relayed_rs.at[way, k - 3, level]
            dst = relayed.at[way, k - 3, level], relayed_step.at[way, k - 3, level]
        else:
            slot = 2 * way + k - 1
            lat, arrived = there, g_rs.at[slot]
            dst = gr.at[slot, level], gr_step.at[slot, level]
        return [send(a, b, g_ss.at[0], arrived, me, lat) for a, b in zip(src, dst)]

    def exists(place):
        return (place >= 0) & (place < nlat)

    def g_first(level):
        for k in range(nlat - 1, 0, -1):
            for way, step in directions:
                ready = exists(z + step * k)
                if k > 1:
                    ready = ready & jnp.logical_not(exists(z - step))

                @pl.when(ready)
                def _():
                    for copy in g_copies(way, step, k, level):
                        copy.start()

    def g_later(level):
        for k in range(nlat - 2, 1, -1):
            for way, step in directions:
                there = z + step * k

                @pl.when(exists(there) & exists(z - step))
                def _():
                    await_bytes(band_bytes, relayed_rs.at[way, k - 2, level])
                    more = decode(relayed[way, k - 2, level], relayed_step[way, k - 2, level])
                    codes, unit = encode((gb[there, level] + more)[None])
                    gq[there, level], gq_step[there, level] = codes[0], unit
                    for copy in g_copies(way, step, k, level):
                        copy.start()

    def backward(level):
        field = jnp.concatenate(
            [
                decode(adjq[level * groups + g], adj_step[level * groups + g]).reshape(urows, flon)
                for g in range(groups)
            ],
            axis=0,
        )
        product = jnp.concatenate(
            [pert_ref[m, level].astype(F32) * field for m in range(members)], axis=0
        )
        hi, lo = split2(product)
        projected = dot(jnp.concatenate([hi, lo], axis=0), lon_t[...])
        projected = projected[: members * rows] + projected[members * rows :]
        projected = jnp.concatenate(
            [projected[m * rows : (m + 1) * rows] for m in range(members)], axis=1
        )
        hi, lo = split2(projected)
        banded = dot(lat_t2, jnp.concatenate([hi, lo], axis=0)).reshape(nlat, cband, width)
        gb[:, level] = banded
        for b in range(nlat):
            codes, unit = encode(banded[b : b + 1])
            gq[b, level], gq_step[b, level] = codes[0], unit
        g_first(level)

    def order(j):
        if groups == 2:
            return pair ^ j
        near_turn = (j == 0) | ((j >= 2) & (j <= npairs))
        i = jnp.where(j < 2, 0, jnp.where(near_turn, j - 1, j - npairs))
        return 2 * (pair ^ i) + jnp.where(near_turn, core, 1 - core)

    def step_back(j):
        backward(order(j))

        @pl.when(j >= LAG)
        def _():
            g_later(order(j - LAG))

    def near(i, carry):
        p = pair ^ i

        @pl.when(i > 0)
        def _():
            await_bytes(unit_bytes, adj_rs.at[p])

        relay(p)
        if groups == 1:
            step_back(jnp.where(i == 0, 0, i + 1))
        return carry

    def far(i, carry):
        p = pair ^ i
        await_bytes(unit_bytes, rel_rs.at[p])
        step_back(jnp.where(i == 0, 1, npairs + i) if groups == 1 else i)
        return carry

    lax.fori_loop(0, 1, near, 0)
    share_increment()
    lax.fori_loop(0, 1, far, 0)
    lax.fori_loop(1, npairs, near, 0)
    lax.fori_loop(1, npairs, far, 0)

    def trail(j, carry):
        g_later(order(j))
        return carry

    lax.fori_loop(lev - LAG, lev, trail, 0)

    inc_all(inc_rs).wait()
    inc_ref[...] = incr[...].reshape(lev * rows, cols)

    for k in range(1, min(3, nlat)):
        for way, step in directions:
            slot = 2 * way + k - 1

            @pl.when(exists(z - step * k))
            def _():
                await_bytes(lev * band_bytes, g_rs.at[slot])
                for level in range(lev):
                    gb[z, level] = gb[z, level] + decode(gr[slot, level], gr_step[slot, level])

    for m in range(members):
        total = jnp.swapaxes(gb[z, :, :, m * clon : (m + 1) * clon], 0, 1)
        total = total * scale
        for c in range(total.shape[0]):
            at = (c * members + m) * lev
            grad_ref[at : at + lev] = total[c] + coarse_ref[c, m].astype(F32)

    def sent(these, sem):
        pltpu.make_async_copy(these, these, sem.at[0]).wait()

    aux_all(aux_ss).wait()
    inc_all(inc_ss).wait()
    sent(pr, pr_ss)
    sent(cg.at[pl.ds(0, nlat - 1)], cg_ss)
    await_bytes((npairs - 1) * unit_bytes, rs_ss.at[0])
    await_bytes((npairs - 1) * unit_bytes, adj_ss.at[0])
    await_bytes(npairs * unit_bytes, rel_ss.at[0])
    await_bytes((nlat - 1) * lev * band_bytes, g_ss.at[0])

    @pl.when(has_up)
    def _():
        ah_up.wait_send()
        await_bytes(npairs * edge_bytes, halo_ss.at[1])

    @pl.when(has_down)
    def _():
        ah_down.wait_send()
        await_bytes(npairs * edge_bytes, halo_ss.at[0])


def finish_kernel(banded_ref, tiles_ref, grad_ref, inc_ref):
    grad_ref[...] = banded_ref[...]
    inc_ref[...] = tiles_ref[...]


def body(
    nmem,
    nlat,
    coarse_weights,
    perturbations,
    lat_matrix,
    lon_matrix,
    wind_field,
    observed_cell,
    observed_value,
    observed_weight,
):
    members, lev, rows, flon = perturbations.shape
    cband, _, _, clon = coarse_weights.shape
    cols = wind_field.shape[2]
    blocks = cols // OBLK
    groups = nmem // lev
    urows = rows // groups
    erows = urows + 2 * HALO
    npairs = nmem // 2
    assert nmem == lev * groups and nmem % 2 == 0 and groups <= 2 and urows % 8 == 0 and urows >= HALO
    assert 2 * cols == LANES and 3 * STEPS * blocks <= LANES
    assert npairs & (npairs - 1) == 0 and HALO == SUB and cband == SUB
    vmem = pl.BlockSpec(memory_space=pltpu.VMEM)
    dma = pltpu.SemaphoreType.DMA
    width = members * clon
    chunks = urows // SUB
    hops = max(1, nlat - 3)
    unit_bytes = urows * flon * 2 + ROW
    band_bytes = cband * width * 2 + ROW
    most = max(npairs * unit_bytes, (nlat - 1) * lev * band_bytes) // ROW
    arguments = (
        coarse_weights,
        perturbations,
        lat_matrix,
        lon_matrix,
        wind_field,
        jnp.swapaxes(observed_cell, 2, 3),
        jnp.swapaxes(observed_value, 2, 3),
        jnp.swapaxes(observed_weight, 2, 3),
    )
    banded, increment = pl.pallas_call(
        functools.partial(kernel, nmem, nlat, float(1.0 / (members * nmem - 1) ** 0.5)),
        out_shape=(
            pltpu.VMEM((cband * members * lev, clon), F32),
            pltpu.VMEM((lev * rows, cols), F32),
        ),
        in_specs=[pl.BlockSpec(memory_space=pltpu.HBM)] * len(arguments),
        out_specs=(vmem, vmem),
        scratch_shapes=[
            *[pltpu.VMEM(x.shape, x.dtype) for x in arguments],
            pltpu.VMEM((lev, rows, 2 * LANES), F32),
            pltpu.VMEM((nlat, lev, members, cband, clon), BF16),
            pltpu.VMEM((nmem, erows, 2 * LANES), F32),
            pltpu.VMEM((nmem, urows, flon), F32),
            pltpu.VMEM((npairs, urows, flon), F32),
            pltpu.VMEM((npairs, chunks, SUB, flon), I16),
            pltpu.VMEM((npairs, 1, LANES), F32),
            pltpu.VMEM((npairs, chunks, SUB, flon), I16),
            pltpu.VMEM((npairs, 1, LANES), F32),
            pltpu.VMEM((2, npairs, SUB, flon), I16),
            pltpu.VMEM((2, npairs, 1, LANES), F32),
            pltpu.VMEM((erows, flon), F32),
            pltpu.VMEM((2 * LANES, 3 * STEPS * LANES), BF16),
            pltpu.VMEM((5, erows, flon), F32),
            pltpu.VMEM((STEPS, erows, flon), F32),
            pltpu.VMEM((STEPS, erows, flon), F32),
            pltpu.VMEM((nmem, urows, cols), F32),
            pltpu.VMEM((lev, rows, cols), F32),
            pltpu.VMEM((nmem, chunks, SUB, flon), I16),
            pltpu.VMEM((nmem, 1, LANES), F32),
            pltpu.VMEM((nlat, lev, cband, width), F32),
            pltpu.VMEM((nlat, lev, cband, width), I16),
            pltpu.VMEM((nlat, lev, 1, LANES), F32),
            pltpu.VMEM((4, lev, cband, width), I16),
            pltpu.VMEM((4, lev, 1, LANES), F32),
            pltpu.VMEM((2, hops, lev, cband, width), I16),
            pltpu.VMEM((2, hops, lev, 1, LANES), F32),
            pltpu.VMEM((flon, clon), BF16),
            pltpu.VMEM((2 * clon, flon), BF16),
            pltpu.VMEM((most, 1, LANES), F32),
            dma((len(arguments),)),
            dma((1,)),
            dma((lev,)),
            dma((1,)),
            dma((1,)),
            dma((2,)),
            dma((2,)),
            dma((1,)),
            dma((npairs,)),
            dma((1,)),
            dma((1,)),
            dma((2,)),
            dma((2,)),
            dma((1,)),
            dma((1,)),
            dma((1,)),
            dma((npairs,)),
            dma((1,)),
            dma((npairs,)),
            dma((1,)),
            dma((4,)),
            dma((2, hops, lev)),
        ],
        compiler_params=pltpu.CompilerParams(
            collective_id=0, has_side_effects=True, vmem_limit_bytes=40 * 1024 * 1024
        ),
    )(*[pltpu.with_memory_space_constraint(x, pltpu.HBM) for x in arguments])
    gradient, increment = pl.pallas_call(
        finish_kernel,
        out_shape=(
            jax.ShapeDtypeStruct((cband * members * lev, clon), F32),
            jax.ShapeDtypeStruct((lev * rows, cols), F32),
        ),
        in_specs=[vmem] * 2,
        out_specs=(vmem, vmem),
        compiler_params=pltpu.CompilerParams(vmem_limit_bytes=4 * 1024 * 1024),
    )(banded, increment)
    return gradient.reshape(coarse_weights.shape), increment.reshape(lev, rows, cols)


def solution(mesh):
    in_specs = (
        P("lat", "mem", None, None),
        P("mem", None, "lat", None),
        P("lat", None),
        P(),
        P(None, "lat", "mem"),
        P(None, None, "lat", "mem"),
        P(None, None, "lat", "mem"),
        P(None, None, "lat", "mem"),
    )
    out_specs = (P("lat", "mem", None, None), P(None, "lat", "mem"))
    call = functools.partial(body, mesh.shape["mem"], mesh.shape["lat"])
    return jax.shard_map(call, mesh=mesh, in_specs=in_specs, out_specs=out_specs, check_vma=False)
```

```python
import functools

import jax
import jax.numpy as jnp
from jax import lax
from jax.experimental import pallas as pl
from jax.experimental.pallas import tpu as pltpu
from jax.sharding import PartitionSpec as P

STEPS = 4
OBLK = 8
HALO = 2 * STEPS
SUB = 8
AUX_AT = 2
DIRECT = 6
LANES = 128
ROW = 4 * LANES
DIFFUSION = 0.2
CODES = 32767.0
WEIGHT_MAX = 4.0
VALUE_MAX = 6.0
WIND_MAX = 0.4
CELL = 4096.0
TINY = 1e-30
F32 = jnp.float32
BF16 = jnp.bfloat16
I16 = jnp.int16


def split2(x):
    hi = x.astype(BF16)
    return hi, (x - hi.astype(F32)).astype(BF16)


def dot(a, b, dims=((1,), (0,))):
    return lax.dot_general(a, b, (dims, ((), ())), preferred_element_type=F32)


def spans(width):
    return [slice(at, at + LANES) for at in range(0, width, LANES)]


def encode(x):
    size = jnp.abs(x)
    peak = functools.reduce(jnp.maximum, [size[i] for i in range(x.shape[0])])
    peak = functools.reduce(jnp.maximum, [peak[:, at] for at in spans(x.shape[2])])
    step = jnp.maximum(jnp.max(peak, axis=0, keepdims=True), TINY) * (1.0 / CODES)
    inverse = 1.0 / step
    scaled = jnp.concatenate([x[:, :, at] * inverse for at in spans(x.shape[2])], axis=2)
    return jnp.round(scaled).astype(jnp.int32).astype(I16), step


def decode(codes, step):
    values = codes.astype(F32)
    return jnp.concatenate([values[..., at] * step for at in spans(codes.shape[-1])], axis=-1)


def kernel(
    nmem,
    nlat,
    scale,
    coarse_hbm,
    pert_hbm,
    lat_hbm,
    lon_hbm,
    wind_hbm,
    cell_hbm,
    value_hbm,
    weight_hbm,
    grad_ref,
    inc_ref,
    coarse_ref,
    pert_ref,
    lat_ref,
    lon_ref,
    wind_ref,
    cell_ref,
    value_ref,
    weight_ref,
    aux_ref,
    cg,
    auxg,
    part,
    pr,
    rq,
    rq_step,
    rs,
    rs_step,
    hq,
    hq_step,
    ext,
    spread,
    coef,
    wts,
    vals,
    itile,
    incr,
    adjq,
    adj_step,
    gb,
    gq,
    gq_step,
    gr,
    gr_step,
    relayed,
    relayed_step,
    lon_t,
    lon_2,
    amount,
    in_sem,
    cg_ss,
    cg_rs,
    aux_ss,
    aux_rs,
    ah_ss,
    ah_rs,
    pr_ss,
    pr_rs,
    rs_ss,
    rs_rs,
    halo_ss,
    halo_rs,
    inc_ss,
    inc_rs,
    adj_ss,
    adj_rs,
    rel_ss,
    rel_rs,
    g_ss,
    g_rs,
    relayed_rs,
):
    members, lev, rows, flon = pert_ref.shape
    clon = lon_ref.shape[0]
    cband, width = gb.shape[2:]
    cols = flon // nmem
    groups = nmem // lev
    urows = rows // groups
    erows = urows + 2 * HALO
    npairs = nmem // 2
    chunks = urows // SUB
    me = lax.axis_index("mem")
    z = lax.axis_index("lat")
    pair = me // 2
    core = me % 2
    partner = pair * 2 + (1 - core)
    my_level = me // groups
    my_group = me % groups
    my_row = my_group * urows
    block = z * groups + my_group
    has_up = block > 0
    has_down = block < nlat * groups - 1
    unit_bytes = urows * flon * 2 + ROW
    edge_bytes = HALO * flon * 2 + ROW
    band_bytes = cband * width * 2 + ROW

    def neighbour(unit, shift):
        there = block + shift
        home = (unit // groups) * groups
        return home + (there + groups) % groups, (there + groups) // groups - 1

    up = neighbour(me, -1)
    down = neighbour(me, 1)

    def send(src, dst, ss, rsem, mem, lat):
        return pltpu.make_async_remote_copy(
            src_ref=src,
            dst_ref=dst,
            send_sem=ss,
            recv_sem=rsem,
            device_id={"mem": mem, "lat": lat},
            device_id_type=pl.DeviceIdType.MESH,
        )

    def await_bytes(count, sem):
        these = amount.at[pl.ds(0, count // ROW)]
        pltpu.make_async_copy(these, these, sem).wait()

    arguments = (
        (coarse_hbm, coarse_ref),
        (lat_hbm, lat_ref),
        (lon_hbm, lon_ref),
        (wind_hbm, wind_ref),
        (cell_hbm, cell_ref),
        (value_hbm, value_ref),
        (weight_hbm, weight_ref),
        (pert_hbm, pert_ref),
    )
    loads = [
        pltpu.make_async_copy(src, dst, in_sem.at[i]) for i, (src, dst) in enumerate(arguments)
    ]
    for load in loads:
        load.start()

    barrier = pltpu.get_barrier_semaphore()

    def greet(mem, lat):
        pl.semaphore_signal(
            barrier, inc=1, device_id={"mem": mem, "lat": lat}, device_id_type=pl.DeviceIdType.MESH
        )

    for i in range(1, nlat):
        greet(me, (z + i) % nlat)
    for i in range(1, nmem):
        greet((me + i) % nmem, z)
    far_up = has_up & (my_group == 0)
    far_down = has_down & (my_group == groups - 1)
    others = range(1, npairs) if groups == 1 else range(npairs)

    def held(i):
        mine = core if i == 0 or groups == 2 else 1 - core
        return 2 * (pair ^ i) + mine, 2 * (pair ^ i) + 1 - mine


    @pl.when(far_up)
    def _():
        for i in others:
            greet(*neighbour(held(i)[0], -1))

    @pl.when(far_down)
    def _():
        for i in others:
            greet(*neighbour(held(i)[0], 1))

    loads[0].wait()
    for m in range(members):
        mine = jnp.swapaxes(coarse_ref[:, m].astype(F32), 0, 1).astype(BF16)
        for level in range(lev):
            cg[z, level, m] = mine[level]
    more = jnp.where(far_up, len(others), 0) + jnp.where(far_down, len(others), 0)
    pl.semaphore_wait(barrier, nmem + nlat - 2 + more)

    if groups == 1:
        turns = [(npairs - 1, True)]
        for i in range(npairs - 1, 0, -1):
            turns += [(i - 1, True), (i, False)]
        turns += [(0, False)]
        levels = [held(i)[1 if theirs else 0] for i, theirs in turns]
        turns_back = [(0, True), (0, False)]
        turns_back += [(i, True) for i in range(1, npairs)]
        turns_back += [(i, False) for i in range(1, npairs)]
        levels_back = [held(i)[0 if mine else 1] for i, mine in turns_back]
    else:
        levels = list(range(lev))
        turns_back = [(i, True) for i in range(npairs)]
        levels_back = [pair ^ i for i in range(npairs)]

    def exists(place):
        return (place >= 0) & (place < nlat)

    directions = ((0, 1), (1, -1))

    for level in levels:
        for k in range(nlat - 1, 0, -1):
            for _, step in directions:
                there = z + step * k

                @pl.when(exists(there))
                def _():
                    block_here = cg.at[z, level]
                    send(block_here, block_here, cg_ss.at[0], cg_rs.at[level], me, there).start()

    def await_coarse(level):
        these = cg.at[pl.ds(0, nlat - 1), level]
        pltpu.make_async_copy(these, these, cg_rs.at[level]).wait()

    for load in loads[1:-1]:
        load.wait()

    blank = jnp.zeros((LANES - 3 * STEPS * (cols // OBLK), rows), F32)
    spot = lax.broadcasted_iota(jnp.int32, (rows, LANES), 1) // (STEPS * (cols // OBLK))
    units = jnp.where(spot == 0, CODES / WEIGHT_MAX, jnp.where(spot == 1, CODES / VALUE_MAX, CELL))

    def coded(x):
        return jnp.round(x).astype(jnp.int32).astype(I16).reshape(rows // SUB, SUB, LANES)

    winds = coded(jnp.concatenate([wind_ref[0], wind_ref[1]], axis=1) * (CODES / WIND_MAX))

    def pack(level, carry):
        pieces = [ref[t, level] for ref in (weight_ref, value_ref) for t in range(STEPS)]
        pieces += [cell_ref[t, level].astype(F32) for t in range(STEPS)]
        seen = jnp.transpose(jnp.concatenate(pieces + [blank], axis=0)) * units
        aux_ref[level, :, :, :LANES] = coded(seen)
        aux_ref[level, :, :, LANES:] = winds
        return carry

    lax.fori_loop(0, lev, pack, 0)

    def aux_copy(there):
        return send(
            aux_ref.at[there // groups, pl.ds((there % groups) * chunks, chunks)],
            auxg.at[me, pl.ds(1, chunks)],
            aux_ss.at[0],
            aux_rs.at[0],
            there,
            z,
        )

    def aux_all(sem):
        these = auxg.at[pl.ds(0, nmem - 1), pl.ds(1, chunks)]
        return pltpu.make_async_copy(these, these, sem.at[0])

    for i in range(1, nmem):
        aux_copy((me + i) % nmem).start()

    auxg[me, 1 : 1 + chunks] = aux_ref[my_level, pl.ds(my_group * chunks, chunks)]

    @pl.when(jnp.logical_not(has_up))
    def _():
        auxg[:, :1] = jnp.zeros((nmem, 1, SUB, 2 * LANES), I16)
        ext[:HALO] = jnp.zeros((HALO, flon), F32)

    @pl.when(jnp.logical_not(has_down))
    def _():
        auxg[:, 1 + chunks :] = jnp.zeros((nmem, 1, SUB, 2 * LANES), I16)
        ext[HALO + urows :] = jnp.zeros((HALO, flon), F32)

    per_tile = cols // OBLK
    k = lax.broadcasted_iota(jnp.int32, (2 * LANES, LANES), 0)
    n = lax.broadcasted_iota(jnp.int32, (2 * LANES, LANES), 1)
    for piece in range(3 * STEPS):
        hit = k == (n // cols) * LANES + piece * per_tile + (n % cols) // OBLK
        spread[:, piece * LANES : (piece + 1) * LANES] = jnp.where(hit, 1.0, 0.0).astype(BF16)

    lat_f32 = lat_ref[...].astype(F32)
    lat_bf = lat_ref[...]
    lat_t = jnp.transpose(lat_f32).astype(BF16)
    lat_t2 = jnp.concatenate([lat_t, lat_t], axis=1)
    lon = lon_ref[...]
    lon_t[...] = jnp.transpose(lon.astype(F32)).astype(BF16)
    lon_2[:clon] = lon
    lon_2[clon:] = lon

    loads[-1].wait()

    def pr_copy(i):
        p = pair ^ i
        return send(part.at[held(i)[1]], pr.at[p], pr_ss.at[0], pr_rs.at[p], partner, z)

    def pr_copy_of(p):
        return send(part.at[2 * p + 1 - core], pr.at[p], pr_ss.at[0], pr_rs.at[p], partner, z)

    def rs_copies(i):
        unit = held(i)[0]
        return (
            send(rq.at[pair ^ i], rs.at[pair], rs_ss.at[0], rs_rs.at[0], unit, z),
            send(rq_step.at[pair ^ i], rs_step.at[pair], rs_ss.at[0], rs_rs.at[0], unit, z),
        )

    def halo_copies(i, side):
        mem, lat = neighbour(held(i)[0], 1 if side == 0 else -1)
        rim = chunks - 1 if side == 0 else 0
        sems = halo_ss.at[side], halo_rs.at[side]
        return (
            send(rq.at[pair ^ i, rim], hq.at[side, pair], *sems, mem, lat),
            send(rq_step.at[pair ^ i], hq_step.at[side, pair], *sems, mem, lat),
        )

    def combine(*places):
        for i in places:
            pr_copy(i).wait_recv()
        for i in places:
            p = pair ^ i
            whole = pr[p] + part[held(i)[0]]
            pr[p] = whole
            rq[p], rq_step[p] = encode(whole.reshape(chunks, SUB, flon))
        for i in places:
            if i:
                for copy in rs_copies(i):
                    copy.start()

        @pl.when(has_down)
        def _():
            for i in places:
                for copy in halo_copies(i, 0):
                    copy.start()

        @pl.when(has_up)
        def _():
            for i in places:
                for copy in halo_copies(i, 1):
                    copy.start()

    ah_up = send(
        auxg.at[:, 1], auxg.at[:, 1 + chunks], ah_ss.at[0], ah_rs.at[0], *up
    )
    ah_down = send(auxg.at[:, chunks], auxg.at[:, 0], ah_ss.at[1], ah_rs.at[1], *down)

    def exchange_aux():
        aux_all(aux_rs).wait()

        @pl.when(has_up)
        def _():
            ah_up.start()

        @pl.when(has_down)
        def _():
            ah_down.start()

    def forward(level):
        coarse = jnp.concatenate(
            [cg[:, level, m].astype(F32).reshape(-1, clon) for m in range(members)], axis=1
        ).astype(BF16)
        partly = dot(lat_bf, coarse)
        partly = jnp.concatenate(
            [partly[:, m * clon : (m + 1) * clon] for m in range(members)], axis=0
        )
        localized = dot(jnp.concatenate(split2(partly), axis=1), lon_2[...])
        total = localized[:rows] * pert_ref[0, level].astype(F32)
        for m in range(1, members):
            total += localized[m * rows : (m + 1) * rows] * pert_ref[m, level].astype(F32)
        part[pl.ds(level * groups, groups)] = total.reshape(groups, urows, flon)

    for at in range(0, lev, 2):
        both = at, at + 1
        for i in both:
            await_coarse(levels[i])
        for i in both:
            forward(levels[i])
        if groups == 1:
            for i in both:
                if turns[i][1]:
                    pr_copy(turns[i][0]).start()
        else:
            for i in both:
                pr_copy_of(levels[i]).start()
        if at == AUX_AT:
            exchange_aux()
        if groups == 1:
            ours = [turns[i][0] for i in both if not turns[i][1]]
            if ours:
                combine(*ours)

    if groups > 1:
        for i in range(npairs - 1, 0, -2):
            combine(i, i - 1)

    rim = auxg.at[:, 0]

    @pl.when(has_down)
    def _():
        pltpu.make_async_copy(rim, rim, ah_rs.at[0]).wait()

    @pl.when(has_up)
    def _():
        pltpu.make_async_copy(rim, rim, ah_rs.at[1]).wait()

    place = block * urows - HALO + lax.broadcasted_iota(jnp.int32, (erows, LANES), 0)
    inside = (place >= 0) & (place < nlat * rows)
    lane = lax.broadcasted_iota(jnp.int32, (erows, LANES), 1)
    tiles = LANES // cols
    for q in range(flon // LANES):
        first, second = (
            auxg[tiles * q + i].astype(F32).reshape(erows, 2 * LANES) for i in range(2)
        )
        lhs = jnp.concatenate([first[:, :LANES], second[:, :LANES]], axis=1)
        upper = jnp.floor(lhs * (1.0 / 256.0))
        lower = lhs - 256.0 * upper
        out = dot(jnp.concatenate([upper.astype(BF16), lower.astype(BF16)], axis=0), spread[...])
        out = 256.0 * out[:erows] + out[erows:]
        at = slice(q * LANES, (q + 1) * LANES)
        for t in range(STEPS):
            weight = out[:, t * LANES : (t + 1) * LANES]
            value = out[:, (STEPS + t) * LANES : (STEPS + t + 1) * LANES]
            cell = out[:, (2 * STEPS + t) * LANES : (2 * STEPS + t + 1) * LANES]
            hit = cell == CELL * (lane % OBLK).astype(F32)
            wts[t, :, at] = jnp.where(hit, weight * (WEIGHT_MAX / CODES), 0.0)
            vals[t, :, at] = value * (VALUE_MAX / CODES)
        w0, w1 = (w[:, LANES:] * (WIND_MAX / CODES) for w in (first, second))
        left = lane < cols
        c0 = jnp.where(left, w0, pltpu.roll(w1, cols, 1))
        c1 = jnp.where(left, pltpu.roll(w0, cols, 1), w1)
        east_in = inside & (lane + q * LANES < flon - 1)
        west_in = inside & (lane + q * LANES > 0)
        coef[0, :, at] = jnp.where(inside, DIFFUSION - 0.5 * c1, 0.0)
        coef[1, :, at] = jnp.where(inside, DIFFUSION + 0.5 * c1, 0.0)
        coef[2, :, at] = jnp.where(east_in, DIFFUSION - 0.5 * c0, 0.0)
        coef[3, :, at] = jnp.where(west_in, DIFFUSION + 0.5 * c0, 0.0)
        coef[4, :, at] = jnp.where(inside, jnp.full((erows, LANES), 1.0 - 4.0 * DIFFUSION, F32), 0.0)

    await_bytes((npairs - 1) * unit_bytes, rs_rs.at[0])
    total = pr[pair]
    for i in range(1, npairs):
        p = pair ^ i
        total = total + decode(rs[p], rs_step[p]).reshape(urows, flon)
    total = total * scale
    ext[HALO : HALO + urows] = total

    def rim_total(side):
        await_bytes(npairs * edge_bytes, halo_rs.at[side])
        return sum(decode(hq[side, p], hq_step[side, p]) for p in range(npairs)) * scale

    @pl.when(has_up)
    def _():
        ext[:HALO] = rim_total(0)

    @pl.when(has_down)
    def _():
        ext[HALO + urows :] = rim_total(1)

    state = ext[...]
    for t in range(STEPS):
        state = (
            coef[4] * state
            + coef[0] * pltpu.roll(state, erows - 1, 0)
            + coef[1] * pltpu.roll(state, 1, 0)
            + coef[2] * pltpu.roll(state, flon - 1, 1)
            + coef[3] * pltpu.roll(state, 1, 1)
        )
        wts[t] = wts[t] * (state - vals[t])
    adjoint = None
    for t in reversed(range(STEPS)):
        adjoint = wts[t] if adjoint is None else adjoint + wts[t]
        adjoint = (
            coef[4] * adjoint
            + pltpu.roll(coef[1] * adjoint, erows - 1, 0)
            + pltpu.roll(coef[0] * adjoint, 1, 0)
            + pltpu.roll(coef[3] * adjoint, flon - 1, 1)
            + pltpu.roll(coef[2] * adjoint, 1, 1)
        )
    adjq[me], adj_step[me] = encode(
        adjoint[HALO : HALO + urows].reshape(urows // SUB, SUB, flon)
    )

    def unit_copies(unit, ss, rsem, mem):
        return (
            send(adjq.at[unit], adjq.at[unit], ss, rsem, mem, z),
            send(adj_step.at[unit], adj_step.at[unit], ss, rsem, mem, z),
        )

    def share_adjoint(i):
        for copy in unit_copies(me, adj_ss.at[0], adj_rs.at[pair], held(i)[0]):
            copy.start()

    for i in range(npairs - 1, 0, -1):
        share_adjoint(i)

    def relay(i):
        for copy in unit_copies(held(i)[0], rel_ss.at[0], rel_rs.at[pair ^ i], partner):
            copy.start()

    def inc_copy(there):
        return send(
            itile.at[there],
            incr.at[my_level, pl.ds(pl.multiple_of(my_row, 8), urows)],
            inc_ss.at[0],
            inc_rs.at[0],
            there,
            z,
        )

    def inc_all(sem):
        these = itile.at[pl.ds(0, nmem - 1)]
        return pltpu.make_async_copy(these, these, sem.at[0])

    def share_increment():
        for m in range(nmem):
            itile[m] = ext[HALO : HALO + urows, m * cols : (m + 1) * cols]
        for i in range(1, nmem):
            inc_copy((me + i) % nmem).start()
        incr[my_level, pl.ds(pl.multiple_of(my_row, 8), urows)] = itile[me]

    direct = DIRECT if nlat == 4 else 0
    reach = 3 if direct else 2

    def g_copies(way, step, k, level, straight):
        there = z + step * k
        src = gq.at[there, level], gq_step.at[there, level]
        if k > 2 and not straight:
            lat, arrived = z + step, relayed_rs.at[way, k - 3, level]
            dst = relayed.at[way, k - 3, level], relayed_step.at[way, k - 3, level]
        else:
            slot = reach * way + k - 1
            lat, arrived = there, g_rs.at[slot]
            dst = gr.at[slot, level], gr_step.at[slot, level]
        return [send(a, b, g_ss.at[0], arrived, me, lat) for a, b in zip(src, dst)]

    def g_start(level, straight, distances):
        for k in distances:
            for way, step in directions:
                ready = exists(z + step * k)
                if k > 1 and not straight:
                    ready = ready & jnp.logical_not(exists(z - step))

                @pl.when(ready)
                def _():
                    for copy in g_copies(way, step, k, level, straight):
                        copy.start()

    def g_later(level):
        for k in range(nlat - 2, 1, -1):
            for way, step in directions:
                there = z + step * k

                @pl.when(exists(there) & exists(z - step))
                def _():
                    await_bytes(band_bytes, relayed_rs.at[way, k - 2, level])
                    more = decode(relayed[way, k - 2, level], relayed_step[way, k - 2, level])
                    codes, unit = encode((gb[there, level] + more)[None])
                    gq[there, level], gq_step[there, level] = codes[0], unit
                    for copy in g_copies(way, step, k, level, False):
                        copy.start()

    def backward(level):
        field = jnp.concatenate(
            [
                decode(adjq[level * groups + g], adj_step[level * groups + g]).reshape(urows, flon)
                for g in range(groups)
            ],
            axis=0,
        )
        product = jnp.concatenate(
            [pert_ref[m, level].astype(F32) * field for m in range(members)], axis=0
        )
        hi, lo = split2(product)
        projected = dot(jnp.concatenate([hi, lo], axis=0), lon_t[...])
        projected = projected[: members * rows] + projected[members * rows :]
        projected = jnp.concatenate(
            [projected[m * rows : (m + 1) * rows] for m in range(members)], axis=1
        )
        hi, lo = split2(projected)
        banded = dot(lat_t2, jnp.concatenate([hi, lo], axis=0)).reshape(nlat, cband, width)
        gb[:, level] = banded
        for b in range(nlat):
            codes, unit = encode(banded[b : b + 1])
            gq[b, level], gq_step[b, level] = codes[0], unit

    def take(i):
        if i:
            await_bytes(unit_bytes, adj_rs.at[pair ^ i])
        relay(i)

    def taken(i):
        await_bytes(unit_bytes, rel_rs.at[pair ^ i])

    if groups == 1:
        batches = [(0,), (1,)] + [(j, j + 1) for j in range(2, lev, 2)]
    else:
        batches = [(j, j + 1) for j in range(0, lev, 2)]

    def later(batch):
        for j in batch:
            if j < lev - direct:
                g_later(levels_back[j])

    def nearest(batch):
        for j in batch:
            g_start(levels_back[j], True, (1,))

    for b, batch in enumerate(batches):
        if groups == 2:
            for j in batch:
                take(j)
            for j in batch:
                taken(j)
        else:
            if b == 0:
                take(0)
            if b == 2:
                for i in range(1, npairs):
                    take(i)
            for j in batch:
                if not turns_back[j][1]:
                    taken(turns_back[j][0])
        for j in batch:
            backward(levels_back[j])
        for j in batch:
            g_start(levels_back[j], j >= lev - direct, range(nlat - 1, 1, -1))
        if b < 2:
            nearest(batch)
        if b == 2:
            share_increment()
            later(batches[0])
        if b > 2:
            nearest(batches[b - 1])
            later(batches[b - 2])
    nearest(batches[-1])
    for batch in batches[-2:]:
        later(batch)

    inc_all(inc_rs).wait()
    inc_ref[...] = incr[...].reshape(lev * rows, cols)

    for k in range(1, reach + 1):
        for way, step in directions:
            slot = reach * way + k - 1
            first = 0 if k < 3 else lev - direct

            @pl.when(exists(z - step * k))
            def _():
                await_bytes((lev - first) * band_bytes, g_rs.at[slot])
                for j in range(first, lev):
                    level = levels_back[j] if first else j
                    gb[z, level] = gb[z, level] + decode(gr[slot, level], gr_step[slot, level])

    for m in range(members):
        total = jnp.swapaxes(gb[z, :, :, m * clon : (m + 1) * clon], 0, 1)
        total = total * scale
        for c in range(total.shape[0]):
            at = (c * members + m) * lev
            grad_ref[at : at + lev] = total[c] + coarse_ref[c, m].astype(F32)

    def sent(these, sem):
        pltpu.make_async_copy(these, these, sem.at[0]).wait()

    aux_all(aux_ss).wait()
    inc_all(inc_ss).wait()
    sent(pr, pr_ss)
    sent(cg.at[pl.ds(0, nlat - 1)], cg_ss)
    await_bytes((npairs - 1) * unit_bytes, rs_ss.at[0])
    await_bytes((npairs - 1) * unit_bytes, adj_ss.at[0])
    await_bytes(npairs * unit_bytes, rel_ss.at[0])
    await_bytes((nlat - 1) * lev * band_bytes, g_ss.at[0])

    @pl.when(has_up)
    def _():
        ah_up.wait_send()
        await_bytes(npairs * edge_bytes, halo_ss.at[1])

    @pl.when(has_down)
    def _():
        ah_down.wait_send()
        await_bytes(npairs * edge_bytes, halo_ss.at[0])


def finish_kernel(banded_ref, tiles_ref, grad_ref, inc_ref):
    grad_ref[...] = banded_ref[...]
    inc_ref[...] = tiles_ref[...]


def body(
    nmem,
    nlat,
    coarse_weights,
    perturbations,
    lat_matrix,
    lon_matrix,
    wind_field,
    observed_cell,
    observed_value,
    observed_weight,
):
    members, lev, rows, flon = perturbations.shape
    cband, _, _, clon = coarse_weights.shape
    cols = wind_field.shape[2]
    blocks = cols // OBLK
    groups = nmem // lev
    urows = rows // groups
    erows = urows + 2 * HALO
    npairs = nmem // 2
    assert nmem == lev * groups and nmem % 2 == 0 and groups <= 2 and urows % 8 == 0 and urows >= HALO
    assert 2 * cols == LANES and 3 * STEPS * blocks <= LANES
    assert npairs & (npairs - 1) == 0 and HALO == SUB and cband == SUB
    vmem = pl.BlockSpec(memory_space=pltpu.VMEM)
    dma = pltpu.SemaphoreType.DMA
    width = members * clon
    chunks = urows // SUB
    hops = max(1, nlat - 3)
    unit_bytes = urows * flon * 2 + ROW
    band_bytes = cband * width * 2 + ROW
    most = max(npairs * unit_bytes, (nlat - 1) * lev * band_bytes) // ROW
    arguments = (
        coarse_weights,
        perturbations,
        lat_matrix,
        lon_matrix,
        wind_field,
        jnp.swapaxes(observed_cell, 2, 3),
        jnp.swapaxes(observed_value, 2, 3),
        jnp.swapaxes(observed_weight, 2, 3),
    )
    banded, increment = pl.pallas_call(
        functools.partial(kernel, nmem, nlat, float(1.0 / (members * nmem - 1) ** 0.5)),
        out_shape=(
            pltpu.VMEM((cband * members * lev, clon), F32),
            pltpu.VMEM((lev * rows, cols), F32),
        ),
        in_specs=[pl.BlockSpec(memory_space=pltpu.HBM)] * len(arguments),
        out_specs=(vmem, vmem),
        scratch_shapes=[
            *[pltpu.VMEM(x.shape, x.dtype) for x in arguments],
            pltpu.VMEM((lev, rows // SUB, SUB, 2 * LANES), I16),
            pltpu.VMEM((nlat, lev, members, cband, clon), BF16),
            pltpu.VMEM((nmem, erows // SUB, SUB, 2 * LANES), I16),
            pltpu.VMEM((nmem, urows, flon), F32),
            pltpu.VMEM((npairs, urows, flon), F32),
            pltpu.VMEM((npairs, chunks, SUB, flon), I16),
            pltpu.VMEM((npairs, 1, LANES), F32),
            pltpu.VMEM((npairs, chunks, SUB, flon), I16),
            pltpu.VMEM((npairs, 1, LANES), F32),
            pltpu.VMEM((2, npairs, SUB, flon), I16),
            pltpu.VMEM((2, npairs, 1, LANES), F32),
            pltpu.VMEM((erows, flon), F32),
            pltpu.VMEM((2 * LANES, 3 * STEPS * LANES), BF16),
            pltpu.VMEM((5, erows, flon), F32),
            pltpu.VMEM((STEPS, erows, flon), F32),
            pltpu.VMEM((STEPS, erows, flon), F32),
            pltpu.VMEM((nmem, urows, cols), F32),
            pltpu.VMEM((lev, rows, cols), F32),
            pltpu.VMEM((nmem, chunks, SUB, flon), I16),
            pltpu.VMEM((nmem, 1, LANES), F32),
            pltpu.VMEM((nlat, lev, cband, width), F32),
            pltpu.VMEM((nlat, lev, cband, width), I16),
            pltpu.VMEM((nlat, lev, 1, LANES), F32),
            pltpu.VMEM((6, lev, cband, width), I16),
            pltpu.VMEM((6, lev, 1, LANES), F32),
            pltpu.VMEM((2, hops, lev, cband, width), I16),
            pltpu.VMEM((2, hops, lev, 1, LANES), F32),
            pltpu.VMEM((flon, clon), BF16),
            pltpu.VMEM((2 * clon, flon), BF16),
            pltpu.VMEM((most, 1, LANES), F32),
            dma((len(arguments),)),
            dma((1,)),
            dma((lev,)),
            dma((1,)),
            dma((1,)),
            dma((2,)),
            dma((2,)),
            dma((1,)),
            dma((npairs,)),
            dma((1,)),
            dma((1,)),
            dma((2,)),
            dma((2,)),
            dma((1,)),
            dma((1,)),
            dma((1,)),
            dma((npairs,)),
            dma((1,)),
            dma((npairs,)),
            dma((1,)),
            dma((6,)),
            dma((2, hops, lev)),
        ],
        compiler_params=pltpu.CompilerParams(
            collective_id=0, has_side_effects=True, vmem_limit_bytes=40 * 1024 * 1024
        ),
    )(*[pltpu.with_memory_space_constraint(x, pltpu.HBM) for x in arguments])
    gradient, increment = pl.pallas_call(
        finish_kernel,
        out_shape=(
            jax.ShapeDtypeStruct((cband * members * lev, clon), F32),
            jax.ShapeDtypeStruct((lev * rows, cols), F32),
        ),
        in_specs=[vmem] * 2,
        out_specs=(vmem, vmem),
        compiler_params=pltpu.CompilerParams(vmem_limit_bytes=4 * 1024 * 1024),
    )(banded, increment)
    return gradient.reshape(coarse_weights.shape), increment.reshape(lev, rows, cols)


def solution(mesh):
    in_specs = (
        P("lat", "mem", None, None),
        P("mem", None, "lat", None),
        P("lat", None),
        P(),
        P(None, "lat", "mem"),
        P(None, None, "lat", "mem"),
        P(None, None, "lat", "mem"),
        P(None, None, "lat", "mem"),
    )
    out_specs = (P("lat", "mem", None, None), P(None, "lat", "mem"))
    call = functools.partial(body, mesh.shape["mem"], mesh.shape["lat"])
    return jax.shard_map(call, mesh=mesh, in_specs=in_specs, out_specs=out_specs, check_vma=False)
```

```python
import functools

import jax
import jax.numpy as jnp
from jax import lax
from jax.experimental import pallas as pl
from jax.experimental.pallas import tpu as pltpu
from jax.sharding import PartitionSpec as P

STEPS = 4
OBLK = 8
HALO = 2 * STEPS
SUB = 8
AUX_AT = 0
REACH = 3
LANES = 128
ROW = 4 * LANES
DIFFUSION = 0.2
CODES = 32767.0
WEIGHT_MAX = 4.0
VALUE_MAX = 6.0
WIND_MAX = 0.4
CELL = 4096.0
TINY = 1e-30
F32 = jnp.float32
BF16 = jnp.bfloat16
I16 = jnp.int16


def split2(x):
    hi = x.astype(BF16)
    return hi, (x - hi.astype(F32)).astype(BF16)


def dot(a, b, dims=((1,), (0,))):
    return lax.dot_general(a, b, (dims, ((), ())), preferred_element_type=F32)


def spans(width):
    return [slice(at, at + LANES) for at in range(0, width, LANES)]


def encode(x):
    size = jnp.abs(x)
    peak = functools.reduce(jnp.maximum, [size[i] for i in range(x.shape[0])])
    peak = functools.reduce(jnp.maximum, [peak[:, at] for at in spans(x.shape[2])])
    step = jnp.maximum(jnp.max(peak, axis=0, keepdims=True), TINY) * (1.0 / CODES)
    inverse = 1.0 / step
    scaled = jnp.concatenate([x[:, :, at] * inverse for at in spans(x.shape[2])], axis=2)
    return jnp.round(scaled).astype(jnp.int32).astype(I16), step


def decode(codes, step):
    values = codes.astype(F32)
    return jnp.concatenate([values[..., at] * step for at in spans(codes.shape[-1])], axis=-1)


def kernel(
    nmem,
    nlat,
    scale,
    all_bytes,
    coarse_hbm,
    pert_hbm,
    lat_hbm,
    lon_hbm,
    wind_hbm,
    cell_hbm,
    value_hbm,
    weight_hbm,
    grad_ref,
    inc_ref,
    coarse_ref,
    pert_ref,
    lat_ref,
    lon_ref,
    wind_ref,
    cell_ref,
    value_ref,
    weight_ref,
    aux_ref,
    cg,
    auxg,
    part,
    pr,
    rq,
    rq_step,
    rs,
    rs_step,
    hq,
    hq_step,
    ext,
    spread,
    coef,
    wts,
    vals,
    itile,
    incr,
    adjq,
    adj_step,
    gb,
    gq,
    gq_step,
    gr,
    gr_step,
    relayed,
    relayed_step,
    lon_t,
    lon_2,
    amount,
    gsum,
    in_sem,
    cg_rs,
    aux_rs,
    ah_rs,
    pr_rs,
    rs_rs,
    halo_rs,
    inc_rs,
    adj_rs,
    rel_rs,
    g_rs,
    relayed_rs,
):
    members, lev, rows, flon = pert_ref.shape
    clon = lon_ref.shape[0]
    cband, width = gb.shape[2:]
    cols = flon // nmem
    groups = nmem // lev
    urows = rows // groups
    erows = urows + 2 * HALO
    npairs = nmem // 2
    chunks = urows // SUB
    me = lax.axis_index("mem")
    z = lax.axis_index("lat")
    pair = me // 2
    core = me % 2
    partner = pair * 2 + (1 - core)
    my_level = me // groups
    my_group = me % groups
    my_row = my_group * urows
    block = z * groups + my_group
    has_up = block > 0
    has_down = block < nlat * groups - 1
    unit_bytes = urows * flon * 2 + ROW
    edge_bytes = HALO * flon * 2 + ROW
    band_bytes = cband * width * 2 + ROW

    def neighbour(unit, shift):
        there = block + shift
        home = (unit // groups) * groups
        return home + (there + groups) % groups, (there + groups) // groups - 1

    up = neighbour(me, -1)
    down = neighbour(me, 1)

    def send(src, dst, ss, rsem, mem, lat):
        return pltpu.make_async_remote_copy(
            src_ref=src,
            dst_ref=dst,
            send_sem=ss,
            recv_sem=rsem,
            device_id={"mem": mem, "lat": lat},
            device_id_type=pl.DeviceIdType.MESH,
        )

    def await_bytes(count, sem):
        these = amount.at[pl.ds(0, count // ROW)]
        pltpu.make_async_copy(these, these, sem).wait()

    arguments = (
        (coarse_hbm, coarse_ref),
        (lat_hbm, lat_ref),
        (lon_hbm, lon_ref),
        (wind_hbm, wind_ref),
        (cell_hbm, cell_ref),
        (value_hbm, value_ref),
        (weight_hbm, weight_ref),
        (pert_hbm, pert_ref),
    )
    loads = [
        pltpu.make_async_copy(src, dst, in_sem.at[i]) for i, (src, dst) in enumerate(arguments)
    ]
    for load in loads:
        load.start()

    gone, inc_out = in_sem.at[0], in_sem.at[3]
    barrier = pltpu.get_barrier_semaphore()

    def greet(mem, lat):
        pl.semaphore_signal(
            barrier, inc=1, device_id={"mem": mem, "lat": lat}, device_id_type=pl.DeviceIdType.MESH
        )

    for i in range(1, nlat):
        greet(me, (z + i) % nlat)
    for i in range(1, nmem):
        greet((me + i) % nmem, z)
    far_up = has_up & (my_group == 0)
    far_down = has_down & (my_group == groups - 1)
    others = range(1, npairs) if groups == 1 else range(npairs)

    def held(i):
        mine = core if i == 0 or groups == 2 else 1 - core
        return 2 * (pair ^ i) + mine, 2 * (pair ^ i) + 1 - mine


    @pl.when(far_up)
    def _():
        for i in others:
            greet(*neighbour(held(i)[0], -1))

    @pl.when(far_down)
    def _():
        for i in others:
            greet(*neighbour(held(i)[0], 1))

    def position(level):
        if groups > 1:
            return level
        away = pair ^ (level // 2)
        mine = jnp.where(away == 0, core, 1 - core) == level % 2
        theirs = jnp.maximum(0, 2 * (npairs - 1 - away) - 1)
        return jnp.where(mine, jnp.minimum(lev - 1, 2 * (npairs - away)), theirs)

    loads[0].wait()
    for m in range(members):
        mine = jnp.swapaxes(coarse_ref[:, m].astype(F32), 0, 1).astype(BF16)
        for level in range(lev):
            cg[z, position(level), m] = mine[level]
    more = jnp.where(far_up, len(others), 0) + jnp.where(far_down, len(others), 0)
    pl.semaphore_wait(barrier, nmem + nlat - 2 + more)

    if groups == 1:
        turns = [(npairs - 1, True)]
        for i in range(npairs - 1, 0, -1):
            turns += [(i - 1, True), (i, False)]
        turns += [(0, False)]
        levels = [held(i)[1 if theirs else 0] for i, theirs in turns]
        turns_back = [(0, True), (0, False)]
        for mine in (True, False):
            turns_back += [(i, mine) for i in range(1, npairs - 1)]
        turns_back += [(npairs - 1, True), (npairs - 1, False)]
        levels_back = [held(i)[0 if mine else 1] for i, mine in turns_back]
    else:
        levels = list(range(lev))
        turns_back = [(i, True) for i in range(npairs)]
        levels_back = [pair ^ i for i in range(npairs)]

    def exists(place):
        return (place >= 0) & (place < nlat)

    directions = ((0, 1), (1, -1))

    def start(a, distances):
        for k in distances:
            for _, step in directions:
                there = z + step * k

                @pl.when(exists(there))
                def _():
                    two = cg.at[z, pl.ds(2 * a, 2)]
                    send(two, two, gone, cg_rs.at[a], me, there).start()

    last = lev // 2 - 1
    at_end = (z == 0) | (z == nlat - 1)

    @pl.when(at_end)
    def _():
        for a in range(last + 1):
            start(a, range(nlat - 1, 1, -1))
            if a:
                start(a - 1, (1,))
        start(last, (1,))

    @pl.when(jnp.logical_not(at_end))
    def _():
        for a in range(last + 1):
            start(a, range(nlat - 1, 0, -1))

    def await_coarse(a):
        these = cg.at[pl.ds(0, nlat - 1), pl.ds(2 * a, 2)]
        pltpu.make_async_copy(these, these, cg_rs.at[a]).wait()

    for load in loads[1:-1]:
        load.wait()

    blank = jnp.zeros((LANES - 3 * STEPS * (cols // OBLK), rows), F32)
    spot = lax.broadcasted_iota(jnp.int32, (rows, LANES), 1) // (STEPS * (cols // OBLK))
    units = jnp.where(spot == 0, CODES / WEIGHT_MAX, jnp.where(spot == 1, CODES / VALUE_MAX, CELL))

    def coded(x):
        return jnp.round(x).astype(jnp.int32).astype(I16).reshape(rows // SUB, SUB, LANES)

    winds = coded(jnp.concatenate([wind_ref[0], wind_ref[1]], axis=1) * (CODES / WIND_MAX))

    def pack(level, carry):
        pieces = [ref[t, level] for ref in (weight_ref, value_ref) for t in range(STEPS)]
        pieces += [cell_ref[t, level].astype(F32) for t in range(STEPS)]
        seen = jnp.transpose(jnp.concatenate(pieces + [blank], axis=0)) * units
        aux_ref[level, :, :, :LANES] = coded(seen)
        aux_ref[level, :, :, LANES:] = winds
        return carry

    lax.fori_loop(0, lev, pack, 0)

    def aux_copy(there):
        return send(
            aux_ref.at[there // groups, pl.ds((there % groups) * chunks, chunks)],
            auxg.at[me, pl.ds(1, chunks)],
            gone,
            aux_rs.at[0],
            there,
            z,
        )

    def aux_all(sem):
        these = auxg.at[pl.ds(0, nmem - 1), pl.ds(1, chunks)]
        return pltpu.make_async_copy(these, these, sem.at[0])

    for i in range(1, nmem):
        aux_copy((me + i) % nmem).start()

    auxg[me, 1 : 1 + chunks] = aux_ref[my_level, pl.ds(my_group * chunks, chunks)]

    @pl.when(jnp.logical_not(has_up))
    def _():
        auxg[:, :1] = jnp.zeros((nmem, 1, SUB, 2 * LANES), I16)
        ext[:HALO] = jnp.zeros((HALO, flon), F32)

    @pl.when(jnp.logical_not(has_down))
    def _():
        auxg[:, 1 + chunks :] = jnp.zeros((nmem, 1, SUB, 2 * LANES), I16)
        ext[HALO + urows :] = jnp.zeros((HALO, flon), F32)

    per_tile = cols // OBLK
    k = lax.broadcasted_iota(jnp.int32, (2 * LANES, LANES), 0)
    n = lax.broadcasted_iota(jnp.int32, (2 * LANES, LANES), 1)
    for piece in range(3 * STEPS):
        hit = k == (n // cols) * LANES + piece * per_tile + (n % cols) // OBLK
        spread[:, piece * LANES : (piece + 1) * LANES] = jnp.where(hit, 1.0, 0.0).astype(BF16)

    lat_f32 = lat_ref[...].astype(F32)
    lat_bf = lat_ref[...]
    lat_t = jnp.transpose(lat_f32).astype(BF16)
    lat_t2 = jnp.concatenate([lat_t, lat_t], axis=1)
    lon = lon_ref[...]
    lon_t[...] = jnp.transpose(lon.astype(F32)).astype(BF16)
    lon_2[:clon] = lon
    lon_2[clon:] = lon

    loads[-1].wait()

    def pr_copy(i):
        p = pair ^ i
        return send(part.at[held(i)[1]], pr.at[p], gone, pr_rs.at[p], partner, z)

    def pr_copy_of(p):
        return send(part.at[2 * p + 1 - core], pr.at[p], gone, pr_rs.at[p], partner, z)

    def rs_copies(i):
        unit = held(i)[0]
        return (
            send(rq.at[pair ^ i], rs.at[pair], gone, rs_rs.at[0], unit, z),
            send(rq_step.at[pair ^ i], rs_step.at[pair], gone, rs_rs.at[0], unit, z),
        )

    def halo_copies(i, side):
        mem, lat = neighbour(held(i)[0], 1 if side == 0 else -1)
        rim = chunks - 1 if side == 0 else 0
        sems = in_sem.at[2 - side], halo_rs.at[side]
        return (
            send(rq.at[pair ^ i, rim], hq.at[side, pair], *sems, mem, lat),
            send(rq_step.at[pair ^ i], hq_step.at[side, pair], *sems, mem, lat),
        )

    def combine(*places):
        for i in places:
            pr_copy(i).wait_recv()
        for i in places:
            p = pair ^ i
            whole = pr[p] + part[held(i)[0]]
            pr[p] = whole
            rq[p], rq_step[p] = encode(whole.reshape(chunks, SUB, flon))
        for i in places:
            if i:
                for copy in rs_copies(i):
                    copy.start()

        @pl.when(has_down)
        def _():
            for i in places:
                for copy in halo_copies(i, 0):
                    copy.start()

        @pl.when(has_up)
        def _():
            for i in places:
                for copy in halo_copies(i, 1):
                    copy.start()

    ah_up = send(
        auxg.at[:, 1], auxg.at[:, 1 + chunks], in_sem.at[1], ah_rs.at[0], *up
    )
    ah_down = send(auxg.at[:, chunks], auxg.at[:, 0], in_sem.at[2], ah_rs.at[1], *down)

    def exchange_aux():
        aux_all(aux_rs).wait()

        @pl.when(has_up)
        def _():
            ah_up.start()

        @pl.when(has_down)
        def _():
            ah_down.start()

    def forward(i, level):
        coarse = jnp.concatenate(
            [cg[:, i, m].astype(F32).reshape(-1, clon) for m in range(members)], axis=1
        ).astype(BF16)
        partly = dot(lat_bf, coarse)
        partly = jnp.concatenate(
            [partly[:, m * clon : (m + 1) * clon] for m in range(members)], axis=0
        )
        localized = dot(jnp.concatenate(split2(partly), axis=1), lon_2[...])
        total = localized[:rows] * pert_ref[0, level].astype(F32)
        for m in range(1, members):
            total += localized[m * rows : (m + 1) * rows] * pert_ref[m, level].astype(F32)
        part[pl.ds(level * groups, groups)] = total.reshape(groups, urows, flon)

    for at in range(0, lev, 2):
        both = at, at + 1
        await_coarse(at // 2)
        for i in both:
            forward(i, levels[i])
        if groups == 1:
            for i in both:
                if turns[i][1]:
                    pr_copy(turns[i][0]).start()
        else:
            for i in both:
                pr_copy_of(levels[i]).start()
        if at == AUX_AT:
            exchange_aux()
        if groups == 1:
            ours = [turns[i][0] for i in both if not turns[i][1]]
            if ours:
                combine(*ours)

    if groups > 1:
        for i in range(npairs - 1, 0, -2):
            combine(i, i - 1)

    rim = auxg.at[:, 0]

    @pl.when(has_down)
    def _():
        pltpu.make_async_copy(rim, rim, ah_rs.at[0]).wait()

    @pl.when(has_up)
    def _():
        pltpu.make_async_copy(rim, rim, ah_rs.at[1]).wait()

    place = block * urows - HALO + lax.broadcasted_iota(jnp.int32, (erows, LANES), 0)
    inside = (place >= 0) & (place < nlat * rows)
    lane = lax.broadcasted_iota(jnp.int32, (erows, LANES), 1)
    tiles = LANES // cols
    for q in range(flon // LANES):
        first, second = (
            auxg[tiles * q + i].astype(F32).reshape(erows, 2 * LANES) for i in range(2)
        )
        lhs = jnp.concatenate([first[:, :LANES], second[:, :LANES]], axis=1)
        upper = jnp.floor(lhs * (1.0 / 256.0))
        lower = lhs - 256.0 * upper
        out = dot(jnp.concatenate([upper.astype(BF16), lower.astype(BF16)], axis=0), spread[...])
        out = 256.0 * out[:erows] + out[erows:]
        at = slice(q * LANES, (q + 1) * LANES)
        for t in range(STEPS):
            weight = out[:, t * LANES : (t + 1) * LANES]
            value = out[:, (STEPS + t) * LANES : (STEPS + t + 1) * LANES]
            cell = out[:, (2 * STEPS + t) * LANES : (2 * STEPS + t + 1) * LANES]
            hit = cell == CELL * (lane % OBLK).astype(F32)
            wts[t, :, at] = jnp.where(hit, weight * (WEIGHT_MAX / CODES), 0.0)
            vals[t, :, at] = value * (VALUE_MAX / CODES)
        w0, w1 = (w[:, LANES:] * (WIND_MAX / CODES) for w in (first, second))
        left = lane < cols
        c0 = jnp.where(left, w0, pltpu.roll(w1, cols, 1))
        c1 = jnp.where(left, pltpu.roll(w0, cols, 1), w1)
        east_in = inside & (lane + q * LANES < flon - 1)
        west_in = inside & (lane + q * LANES > 0)
        coef[0, :, at] = jnp.where(inside, DIFFUSION - 0.5 * c1, 0.0)
        coef[1, :, at] = jnp.where(inside, DIFFUSION + 0.5 * c1, 0.0)
        coef[2, :, at] = jnp.where(east_in, DIFFUSION - 0.5 * c0, 0.0)
        coef[3, :, at] = jnp.where(west_in, DIFFUSION + 0.5 * c0, 0.0)
        coef[4, :, at] = jnp.where(inside, jnp.full((erows, LANES), 1.0 - 4.0 * DIFFUSION, F32), 0.0)

    await_bytes((npairs - 1) * unit_bytes, rs_rs.at[0])
    total = pr[pair]
    for i in range(1, npairs):
        p = pair ^ i
        total = total + decode(rs[p], rs_step[p]).reshape(urows, flon)
    total = total * scale
    ext[HALO : HALO + urows] = total

    def rim_total(side):
        await_bytes(npairs * edge_bytes, halo_rs.at[side])
        return sum(decode(hq[side, p], hq_step[side, p]) for p in range(npairs)) * scale

    @pl.when(has_up)
    def _():
        ext[:HALO] = rim_total(0)

    @pl.when(has_down)
    def _():
        ext[HALO + urows :] = rim_total(1)

    state = ext[...]
    for t in range(STEPS):
        state = (
            coef[4] * state
            + coef[0] * pltpu.roll(state, erows - 1, 0)
            + coef[1] * pltpu.roll(state, 1, 0)
            + coef[2] * pltpu.roll(state, flon - 1, 1)
            + coef[3] * pltpu.roll(state, 1, 1)
        )
        wts[t] = wts[t] * (state - vals[t])
    adjoint = None
    for t in reversed(range(STEPS)):
        adjoint = wts[t] if adjoint is None else adjoint + wts[t]
        adjoint = (
            coef[4] * adjoint
            + pltpu.roll(coef[1] * adjoint, erows - 1, 0)
            + pltpu.roll(coef[0] * adjoint, 1, 0)
            + pltpu.roll(coef[3] * adjoint, flon - 1, 1)
            + pltpu.roll(coef[2] * adjoint, 1, 1)
        )
    adjq[me], adj_step[me] = encode(
        adjoint[HALO : HALO + urows].reshape(urows // SUB, SUB, flon)
    )

    def unit_copies(unit, ss, rsem, mem):
        return (
            send(adjq.at[unit], adjq.at[unit], ss, rsem, mem, z),
            send(adj_step.at[unit], adj_step.at[unit], ss, rsem, mem, z),
        )

    def share_adjoint(i):
        for copy in unit_copies(me, gone, adj_rs.at[pair], held(i)[0]):
            copy.start()

    for i in range(1, npairs):
        share_adjoint(i)

    def relay(i):
        for copy in unit_copies(held(i)[0], gone, rel_rs.at[pair ^ i], partner):
            copy.start()

    def inc_copy(there):
        return send(
            itile.at[there],
            incr.at[my_level, pl.ds(pl.multiple_of(my_row, 8), urows)],
            inc_out,
            inc_rs.at[0],
            there,
            z,
        )

    def inc_all(sem):
        these = itile.at[pl.ds(0, nmem - 1)]
        return pltpu.make_async_copy(these, these, sem)

    def share_increment():
        for m in range(nmem):
            itile[m] = ext[HALO : HALO + urows, m * cols : (m + 1) * cols]
        for i in range(1, nmem):
            inc_copy((me + i) % nmem).start()
        incr[my_level, pl.ds(pl.multiple_of(my_row, 8), urows)] = itile[me]

    direct = lev if nlat <= REACH + 1 else 0
    reach = REACH if direct else 2

    def g_copies(way, step, k, batch, straight):
        there = z + step * k
        js = pl.ds(batch[0], len(batch))
        src = gq.at[there, js], gq_step.at[there, js]
        if k > 2 and not straight:
            lat, arrived = z + step, relayed_rs.at[way, k - 3, batch[0]]
            dst = relayed.at[way, k - 3, js], relayed_step.at[way, k - 3, js]
        else:
            slot = reach * way + k - 1
            lat, arrived = there, g_rs.at[slot]
            dst = gr.at[slot, js], gr_step.at[slot, js]
        return [send(a, b, gone, arrived, me, lat) for a, b in zip(src, dst)]

    def g_start(batch, straight, distances):
        for k in distances:
            for way, step in directions:
                ready = exists(z + step * k)
                if k > 1 and not straight:
                    ready = ready & jnp.logical_not(exists(z - step))

                @pl.when(ready)
                def _():
                    for copy in g_copies(way, step, k, batch, straight):
                        copy.start()

    def g_later(batch):
        for k in range(nlat - 2, 1, -1):
            for way, step in directions:
                there = z + step * k

                @pl.when(exists(there) & exists(z - step))
                def _():
                    arrived = relayed_rs.at[way, k - 2, batch[0]]
                    await_bytes(len(batch) * band_bytes, arrived)
                    for j in batch:
                        more = decode(relayed[way, k - 2, j], relayed_step[way, k - 2, j])
                        codes, unit = encode((gb[there, j] + more)[None])
                        gq[there, j], gq_step[there, j] = codes[0], unit
                    for copy in g_copies(way, step, k, batch, False):
                        copy.start()

    def backward(j, level):
        field = jnp.concatenate(
            [
                decode(adjq[level * groups + g], adj_step[level * groups + g]).reshape(urows, flon)
                for g in range(groups)
            ],
            axis=0,
        )
        product = jnp.concatenate(
            [pert_ref[m, level].astype(F32) * field for m in range(members)], axis=0
        )
        hi, lo = split2(product)
        projected = dot(jnp.concatenate([hi, lo], axis=0), lon_t[...])
        projected = projected[: members * rows] + projected[members * rows :]
        projected = jnp.concatenate(
            [projected[m * rows : (m + 1) * rows] for m in range(members)], axis=1
        )
        hi, lo = split2(projected)
        banded = dot(lat_t2, jnp.concatenate([hi, lo], axis=0)).reshape(nlat, cband, width)
        gb[:, j] = banded
        for b in range(nlat):
            codes, unit = encode(banded[b : b + 1])
            gq[b, j], gq_step[b, j] = codes[0], unit

    def take(i):
        if i:
            await_bytes(unit_bytes, adj_rs.at[pair ^ i])
        relay(i)

    def taken(i):
        await_bytes(unit_bytes, rel_rs.at[pair ^ i])

    batches = [(j, j + 1) for j in range(0, lev, 2)]
    if groups == 1:
        batches = [(j,) for j in range(lev)]

    def later(batch):
        if batch[0] < lev - direct:
            g_later(batch)

    def nearest(batch):
        g_start(batch, True, (1,))

    for b, batch in enumerate(batches):
        if groups == 2:
            for j in batch:
                take(j)
            for j in batch:
                taken(j)
        else:
            if b == 0:
                take(0)
            if b == 2:
                for i in range(1, npairs - 1):
                    take(i)
            if batch[0] == npairs:
                take(npairs - 1)
            for j in batch:
                if not turns_back[j][1]:
                    taken(turns_back[j][0])
        for j in batch:
            backward(j, levels_back[j])
        g_start(batch, batch[0] >= lev - direct, range(nlat - 1, 1, -1))
        if b < 2:
            nearest(batch)
        if b == 2:
            share_increment()
        if b > 2:
            nearest(batches[b - 1])
        if b > 1:
            later(batches[b - 2])
    nearest(batches[-1])
    for batch in batches[-2:]:
        later(batch)

    inc_all(inc_rs.at[0]).wait()
    inc_ref[...] = incr[...].reshape(lev * rows, cols)

    for k in range(1, reach + 1):
        for way, step in directions:
            slot = reach * way + k - 1
            first = 0 if k < 3 else lev - direct

            @pl.when(exists(z - step * k))
            def _():
                await_bytes((lev - first) * band_bytes, g_rs.at[slot])
                for j in range(first, lev):
                    gb[z, j] = gb[z, j] + decode(gr[slot, j], gr_step[slot, j])

    for j in range(lev):
        gsum[levels_back[j]] = gb[z, j]
    for m in range(members):
        total = jnp.swapaxes(gsum[:, :, m * clon : (m + 1) * clon], 0, 1)
        total = total * scale
        for c in range(total.shape[0]):
            at = (c * members + m) * lev
            grad_ref[at : at + lev] = total[c] + coarse_ref[c, m].astype(F32)

    await_bytes(all_bytes, gone)
    inc_all(inc_out).wait()
    rim_bytes = rim.size * 2 + npairs * edge_bytes

    @pl.when(has_up)
    def _():
        await_bytes(rim_bytes, in_sem.at[1])

    @pl.when(has_down)
    def _():
        await_bytes(rim_bytes, in_sem.at[2])


def finish_kernel(banded_ref, tiles_ref, grad_ref, inc_ref):
    grad_ref[...] = banded_ref[...]
    inc_ref[...] = tiles_ref[...]


def body(
    nmem,
    nlat,
    coarse_weights,
    perturbations,
    lat_matrix,
    lon_matrix,
    wind_field,
    observed_cell,
    observed_value,
    observed_weight,
):
    members, lev, rows, flon = perturbations.shape
    cband, _, _, clon = coarse_weights.shape
    cols = wind_field.shape[2]
    blocks = cols // OBLK
    groups = nmem // lev
    urows = rows // groups
    erows = urows + 2 * HALO
    npairs = nmem // 2
    assert nmem == lev * groups and nmem % 2 == 0 and groups <= 2 and urows % 8 == 0 and urows >= HALO
    assert 2 * cols == LANES and 3 * STEPS * blocks <= LANES
    assert npairs & (npairs - 1) == 0 and HALO == SUB and cband == SUB
    vmem = pl.BlockSpec(memory_space=pltpu.VMEM)
    dma = pltpu.SemaphoreType.DMA
    width = members * clon
    chunks = urows // SUB
    hops = nlat - 3 if nlat > REACH + 1 else 1
    unit_bytes = urows * flon * 2 + ROW
    band_bytes = cband * width * 2 + ROW
    all_bytes = (
        (nlat - 1) * coarse_weights.size * 2
        + (nmem - 1) * urows * 2 * LANES * 2
        + npairs * urows * flon * 4
        + (3 * npairs - 2) * unit_bytes
        + (nlat - 1) * lev * band_bytes
    )
    arguments = (
        coarse_weights,
        perturbations,
        lat_matrix,
        lon_matrix,
        wind_field,
        jnp.swapaxes(observed_cell, 2, 3),
        jnp.swapaxes(observed_value, 2, 3),
        jnp.swapaxes(observed_weight, 2, 3),
    )
    banded, increment = pl.pallas_call(
        functools.partial(
            kernel, nmem, nlat, float(1.0 / (members * nmem - 1) ** 0.5), all_bytes
        ),
        out_shape=(
            pltpu.VMEM((cband * members * lev, clon), F32),
            pltpu.VMEM((lev * rows, cols), F32),
        ),
        in_specs=[pl.BlockSpec(memory_space=pltpu.HBM)] * len(arguments),
        out_specs=(vmem, vmem),
        scratch_shapes=[
            *[pltpu.VMEM(x.shape, x.dtype) for x in arguments],
            pltpu.VMEM((lev, rows // SUB, SUB, 2 * LANES), I16),
            pltpu.VMEM((nlat, lev, members, cband, clon), BF16),
            pltpu.VMEM((nmem, erows // SUB, SUB, 2 * LANES), I16),
            pltpu.VMEM((nmem, urows, flon), F32),
            pltpu.VMEM((npairs, urows, flon), F32),
            pltpu.VMEM((npairs, chunks, SUB, flon), I16),
            pltpu.VMEM((npairs, 1, LANES), F32),
            pltpu.VMEM((npairs, chunks, SUB, flon), I16),
            pltpu.VMEM((npairs, 1, LANES), F32),
            pltpu.VMEM((2, npairs, SUB, flon), I16),
            pltpu.VMEM((2, npairs, 1, LANES), F32),
            pltpu.VMEM((erows, flon), F32),
            pltpu.VMEM((2 * LANES, 3 * STEPS * LANES), BF16),
            pltpu.VMEM((5, erows, flon), F32),
            pltpu.VMEM((STEPS, erows, flon), F32),
            pltpu.VMEM((STEPS, erows, flon), F32),
            pltpu.VMEM((nmem, urows, cols), F32),
            pltpu.VMEM((lev, rows, cols), F32),
            pltpu.VMEM((nmem, chunks, SUB, flon), I16),
            pltpu.VMEM((nmem, 1, LANES), F32),
            pltpu.VMEM((nlat, lev, cband, width), F32),
            pltpu.VMEM((nlat, lev, cband, width), I16),
            pltpu.VMEM((nlat, lev, 1, LANES), F32),
            pltpu.VMEM((6, lev, cband, width), I16),
            pltpu.VMEM((6, lev, 1, LANES), F32),
            pltpu.VMEM((2, hops, lev if nlat > REACH + 1 else 1, cband, width), I16),
            pltpu.VMEM((2, hops, lev if nlat > REACH + 1 else 1, 1, LANES), F32),
            pltpu.VMEM((flon, clon), BF16),
            pltpu.VMEM((2 * clon, flon), BF16),
            pltpu.VMEM((all_bytes // ROW, 1, LANES), F32),
            pltpu.VMEM((lev, cband, width), F32),
            dma((len(arguments),)),
            dma((lev // 2,)),
            dma((1,)),
            dma((2,)),
            dma((npairs,)),
            dma((1,)),
            dma((2,)),
            dma((1,)),
            dma((npairs,)),
            dma((npairs,)),
            dma((6,)),
            dma((2, hops, lev if nlat > REACH + 1 else 1)),
        ],
        compiler_params=pltpu.CompilerParams(
            collective_id=0, has_side_effects=True, vmem_limit_bytes=40 * 1024 * 1024
        ),
    )(*[pltpu.with_memory_space_constraint(x, pltpu.HBM) for x in arguments])
    gradient, increment = pl.pallas_call(
        finish_kernel,
        out_shape=(
            jax.ShapeDtypeStruct((cband * members * lev, clon), F32),
            jax.ShapeDtypeStruct((lev * rows, cols), F32),
        ),
        in_specs=[vmem] * 2,
        out_specs=(vmem, vmem),
        compiler_params=pltpu.CompilerParams(vmem_limit_bytes=4 * 1024 * 1024),
    )(banded, increment)
    return gradient.reshape(coarse_weights.shape), increment.reshape(lev, rows, cols)


def solution(mesh):
    in_specs = (
        P("lat", "mem", None, None),
        P("mem", None, "lat", None),
        P("lat", None),
        P(),
        P(None, "lat", "mem"),
        P(None, None, "lat", "mem"),
        P(None, None, "lat", "mem"),
        P(None, None, "lat", "mem"),
    )
    out_specs = (P("lat", "mem", None, None), P(None, "lat", "mem"))
    call = functools.partial(body, mesh.shape["mem"], mesh.shape["lat"])
    return jax.shard_map(call, mesh=mesh, in_specs=in_specs, out_specs=out_specs, check_vma=False)
```

```python
import functools

import jax
import jax.numpy as jnp
from jax import lax
from jax.experimental import pallas as pl
from jax.experimental.pallas import tpu as pltpu
from jax.sharding import PartitionSpec as P

STEPS = 4
OBLK = 8
HALO = 2 * STEPS
SUB = 8
AUX_AT = 2
REACH = 3
LANES = 128
ROW = 4 * LANES
DIFFUSION = 0.2
CODES = 32767.0
WEIGHT_MAX = 4.0
VALUE_MAX = 6.0
WIND_MAX = 0.4
CELL = 4096.0
TINY = 1e-30
F32 = jnp.float32
BF16 = jnp.bfloat16
I16 = jnp.int16


def split2(x):
    hi = x.astype(BF16)
    return hi, (x - hi.astype(F32)).astype(BF16)


def dot(a, b, dims=((1,), (0,))):
    return lax.dot_general(a, b, (dims, ((), ())), preferred_element_type=F32)


def spans(width):
    return [slice(at, at + LANES) for at in range(0, width, LANES)]


def encode(x):
    size = jnp.abs(x)
    peak = functools.reduce(jnp.maximum, [size[i] for i in range(x.shape[0])])
    peak = functools.reduce(jnp.maximum, [peak[:, at] for at in spans(x.shape[2])])
    step = jnp.maximum(jnp.max(peak, axis=0, keepdims=True), TINY) * (1.0 / CODES)
    inverse = 1.0 / step
    scaled = jnp.concatenate([x[:, :, at] * inverse for at in spans(x.shape[2])], axis=2)
    return jnp.round(scaled).astype(jnp.int32).astype(I16), step


def decode(codes, step):
    values = codes.astype(F32)
    return jnp.concatenate([values[..., at] * step for at in spans(codes.shape[-1])], axis=-1)


def kernel(
    nmem,
    nlat,
    scale,
    all_bytes,
    coarse_hbm,
    pert_hbm,
    lat_hbm,
    lon_hbm,
    wind_hbm,
    cell_hbm,
    value_hbm,
    weight_hbm,
    grad_ref,
    inc_ref,
    coarse_ref,
    pert_ref,
    lat_ref,
    lon_ref,
    wind_ref,
    cell_ref,
    value_ref,
    weight_ref,
    aux_ref,
    cg,
    auxg,
    part,
    pr,
    rq,
    rq_step,
    rs,
    rs_step,
    hq,
    hq_step,
    ext,
    spread,
    coef,
    wts,
    vals,
    itile,
    incr,
    adjq,
    adj_step,
    gb,
    gq,
    gq_step,
    gr,
    gr_step,
    relayed,
    relayed_step,
    lon_t,
    lon_2,
    amount,
    gsum,
    in_sem,
    cg_rs,
    aux_rs,
    ah_rs,
    pr_rs,
    rs_rs,
    halo_rs,
    inc_rs,
    adj_rs,
    rel_rs,
    g_rs,
    relayed_rs,
):
    members, lev, rows, flon = pert_ref.shape
    clon = lon_ref.shape[0]
    cband, width = gb.shape[2:]
    cols = flon // nmem
    groups = nmem // lev
    urows = rows // groups
    erows = urows + 2 * HALO
    npairs = nmem // 2
    chunks = urows // SUB
    me = lax.axis_index("mem")
    z = lax.axis_index("lat")
    pair = me // 2
    core = me % 2
    partner = pair * 2 + (1 - core)
    my_level = me // groups
    my_group = me % groups
    my_row = my_group * urows
    block = z * groups + my_group
    has_up = block > 0
    has_down = block < nlat * groups - 1
    unit_bytes = urows * flon * 2 + ROW
    edge_bytes = HALO * flon * 2 + ROW
    band_bytes = cband * width * 2 + ROW

    def neighbour(unit, shift):
        there = block + shift
        home = (unit // groups) * groups
        return home + (there + groups) % groups, (there + groups) // groups - 1

    up = neighbour(me, -1)
    down = neighbour(me, 1)

    def send(src, dst, ss, rsem, mem, lat):
        return pltpu.make_async_remote_copy(
            src_ref=src,
            dst_ref=dst,
            send_sem=ss,
            recv_sem=rsem,
            device_id={"mem": mem, "lat": lat},
            device_id_type=pl.DeviceIdType.MESH,
        )

    def await_bytes(count, sem):
        these = amount.at[pl.ds(0, count // ROW)]
        pltpu.make_async_copy(these, these, sem).wait()

    arguments = (
        (coarse_hbm, coarse_ref),
        (lat_hbm, lat_ref),
        (lon_hbm, lon_ref),
        (wind_hbm, wind_ref),
        (cell_hbm, cell_ref),
        (value_hbm, value_ref),
        (weight_hbm, weight_ref),
        (pert_hbm, pert_ref),
    )
    loads = [
        pltpu.make_async_copy(src, dst, in_sem.at[i]) for i, (src, dst) in enumerate(arguments)
    ]
    for load in loads:
        load.start()

    gone, inc_out = in_sem.at[0], in_sem.at[3]
    barrier = pltpu.get_barrier_semaphore()

    def greet(mem, lat):
        pl.semaphore_signal(
            barrier, inc=1, device_id={"mem": mem, "lat": lat}, device_id_type=pl.DeviceIdType.MESH
        )

    for i in range(1, nlat):
        greet(me, (z + i) % nlat)
    for i in range(1, nmem):
        greet((me + i) % nmem, z)
    far_up = has_up & (my_group == 0)
    far_down = has_down & (my_group == groups - 1)
    others = range(1, npairs) if groups == 1 else range(npairs)

    def held(i):
        mine = core if i == 0 or groups == 2 else 1 - core
        return 2 * (pair ^ i) + mine, 2 * (pair ^ i) + 1 - mine


    @pl.when(far_up)
    def _():
        for i in others:
            greet(*neighbour(held(i)[0], -1))

    @pl.when(far_down)
    def _():
        for i in others:
            greet(*neighbour(held(i)[0], 1))

    def position(level):
        if groups > 1:
            return level
        away = pair ^ (level // 2)
        mine = jnp.where(away == 0, core, 1 - core) == level % 2
        theirs = jnp.maximum(0, 2 * (npairs - 1 - away) - 1)
        return jnp.where(mine, jnp.minimum(lev - 1, 2 * (npairs - away)), theirs)

    loads[0].wait()
    for m in range(members):
        mine = jnp.swapaxes(coarse_ref[:, m].astype(F32), 0, 1).astype(BF16)
        for level in range(lev):
            cg[z, position(level), m] = mine[level]
    more = jnp.where(far_up, len(others), 0) + jnp.where(far_down, len(others), 0)
    pl.semaphore_wait(barrier, nmem + nlat - 2 + more)

    if groups == 1:
        turns = [(npairs - 1, True)]
        for i in range(npairs - 1, 0, -1):
            turns += [(i - 1, True), (i, False)]
        turns += [(0, False)]
        levels = [held(i)[1 if theirs else 0] for i, theirs in turns]
        turns_back = [(0, True), (0, False)]
        for mine in (True, False):
            turns_back += [(i, mine) for i in range(1, npairs - 1)]
        turns_back += [(npairs - 1, True), (npairs - 1, False)]
        levels_back = [held(i)[0 if mine else 1] for i, mine in turns_back]
    else:
        levels = list(range(lev))
        turns_back = [(i, True) for i in range(npairs)]
        levels_back = [pair ^ i for i in range(npairs)]

    def exists(place):
        return (place >= 0) & (place < nlat)

    directions = ((0, 1), (1, -1))

    def start(a, distances):
        for k in distances:
            for _, step in directions:
                there = z + step * k

                @pl.when(exists(there))
                def _():
                    these = cg.at[z, pl.ds(sets[a][0], len(sets[a]))]
                    send(these, these, gone, cg_rs.at[a], me, there).start()

    sets = [(i, i + 1) for i in range(0, lev, 2)]
    if groups == 1:
        sets = [(i,) for i in range(lev)]
    last = len(sets) - 1
    at_end = (z == 0) | (z == nlat - 1)

    @pl.when(at_end)
    def _():
        for a in range(last + 1):
            start(a, range(nlat - 1, 1, -1))
            if a:
                start(a - 1, (1,))
        start(last, (1,))

    @pl.when(jnp.logical_not(at_end))
    def _():
        for a in range(last + 1):
            start(a, range(nlat - 1, 0, -1))

    def await_coarse(a):
        these = cg.at[pl.ds(0, nlat - 1), pl.ds(sets[a][0], len(sets[a]))]
        pltpu.make_async_copy(these, these, cg_rs.at[a]).wait()

    for load in loads[1:-1]:
        load.wait()

    blank = jnp.zeros((LANES - 3 * STEPS * (cols // OBLK), rows), F32)
    spot = lax.broadcasted_iota(jnp.int32, (rows, LANES), 1) // (STEPS * (cols // OBLK))
    units = jnp.where(spot == 0, CODES / WEIGHT_MAX, jnp.where(spot == 1, CODES / VALUE_MAX, CELL))

    def coded(x):
        return jnp.round(x).astype(jnp.int32).astype(I16).reshape(rows // SUB, SUB, LANES)

    winds = coded(jnp.concatenate([wind_ref[0], wind_ref[1]], axis=1) * (CODES / WIND_MAX))

    def pack(level, carry):
        pieces = [ref[t, level] for ref in (weight_ref, value_ref) for t in range(STEPS)]
        pieces += [cell_ref[t, level].astype(F32) for t in range(STEPS)]
        seen = jnp.transpose(jnp.concatenate(pieces + [blank], axis=0)) * units
        aux_ref[level, :, :, :LANES] = coded(seen)
        aux_ref[level, :, :, LANES:] = winds
        return carry

    lax.fori_loop(0, lev, pack, 0)

    def aux_copy(there):
        return send(
            aux_ref.at[there // groups, pl.ds((there % groups) * chunks, chunks)],
            auxg.at[me, pl.ds(1, chunks)],
            gone,
            aux_rs.at[0],
            there,
            z,
        )

    def aux_all(sem):
        these = auxg.at[pl.ds(0, nmem - 1), pl.ds(1, chunks)]
        return pltpu.make_async_copy(these, these, sem.at[0])

    for i in range(1, nmem):
        aux_copy((me + i) % nmem).start()

    auxg[me, 1 : 1 + chunks] = aux_ref[my_level, pl.ds(my_group * chunks, chunks)]

    @pl.when(jnp.logical_not(has_up))
    def _():
        auxg[:, :1] = jnp.zeros((nmem, 1, SUB, 2 * LANES), I16)
        ext[:HALO] = jnp.zeros((HALO, flon), F32)

    @pl.when(jnp.logical_not(has_down))
    def _():
        auxg[:, 1 + chunks :] = jnp.zeros((nmem, 1, SUB, 2 * LANES), I16)
        ext[HALO + urows :] = jnp.zeros((HALO, flon), F32)

    per_tile = cols // OBLK
    k = lax.broadcasted_iota(jnp.int32, (2 * LANES, LANES), 0)
    n = lax.broadcasted_iota(jnp.int32, (2 * LANES, LANES), 1)
    for piece in range(3 * STEPS):
        hit = k == (n // cols) * LANES + piece * per_tile + (n % cols) // OBLK
        spread[:, piece * LANES : (piece + 1) * LANES] = jnp.where(hit, 1.0, 0.0).astype(BF16)

    lat_f32 = lat_ref[...].astype(F32)
    lat_bf = lat_ref[...]
    lat_t = jnp.transpose(lat_f32).astype(BF16)
    lat_t2 = jnp.concatenate([lat_t, lat_t], axis=1)
    lon = lon_ref[...]
    lon_t[:flon] = jnp.transpose(lon.astype(F32)).astype(BF16)
    lon_t[flon:] = lon_t[:flon]
    lon_2[:clon] = lon
    lon_2[clon:] = lon

    loads[-1].wait()

    def pr_copy(i):
        p = pair ^ i
        return send(part.at[held(i)[1]], pr.at[p], gone, pr_rs.at[p], partner, z)

    def pr_copy_of(p):
        return send(part.at[2 * p + 1 - core], pr.at[p], gone, pr_rs.at[p], partner, z)

    def rs_copies(i):
        unit = held(i)[0]
        return (
            send(rq.at[pair ^ i], rs.at[pair], gone, rs_rs.at[0], unit, z),
            send(rq_step.at[pair ^ i], rs_step.at[pair], gone, rs_rs.at[0], unit, z),
        )

    def halo_copies(i, side):
        mem, lat = neighbour(held(i)[0], 1 if side == 0 else -1)
        rim = chunks - 1 if side == 0 else 0
        sems = in_sem.at[2 - side], halo_rs.at[side]
        return (
            send(rq.at[pair ^ i, rim], hq.at[side, pair], *sems, mem, lat),
            send(rq_step.at[pair ^ i], hq_step.at[side, pair], *sems, mem, lat),
        )

    def combine(*places):
        for i in places:
            pr_copy(i).wait_recv()
        for i in places:
            p = pair ^ i
            whole = pr[p] + part[held(i)[0]]
            pr[p] = whole
            rq[p], rq_step[p] = encode(whole.reshape(chunks, SUB, flon))
        for i in places:
            if i:
                for copy in rs_copies(i):
                    copy.start()

        @pl.when(has_down)
        def _():
            for i in places:
                for copy in halo_copies(i, 0):
                    copy.start()

        @pl.when(has_up)
        def _():
            for i in places:
                for copy in halo_copies(i, 1):
                    copy.start()

    ah_up = send(
        auxg.at[:, 1], auxg.at[:, 1 + chunks], in_sem.at[1], ah_rs.at[0], *up
    )
    ah_down = send(auxg.at[:, chunks], auxg.at[:, 0], in_sem.at[2], ah_rs.at[1], *down)

    def exchange_aux():
        aux_all(aux_rs).wait()

        @pl.when(has_up)
        def _():
            ah_up.start()

        @pl.when(has_down)
        def _():
            ah_down.start()

    def forward(i, level):
        coarse = jnp.concatenate(
            [cg[:, i, m].astype(F32).reshape(-1, clon) for m in range(members)], axis=1
        ).astype(BF16)
        partly = dot(lat_bf, coarse)
        partly = jnp.concatenate(
            [partly[:, m * clon : (m + 1) * clon] for m in range(members)], axis=0
        )
        localized = dot(jnp.concatenate(split2(partly), axis=1), lon_2[...])
        total = localized[:rows] * pert_ref[0, level].astype(F32)
        for m in range(1, members):
            total += localized[m * rows : (m + 1) * rows] * pert_ref[m, level].astype(F32)
        part[pl.ds(level * groups, groups)] = total.reshape(groups, urows, flon)

    for at, both in enumerate(sets):
        await_coarse(at)
        for i in both:
            forward(i, levels[i])
        if groups == 1:
            for i in both:
                if turns[i][1]:
                    pr_copy(turns[i][0]).start()
        else:
            for i in both:
                pr_copy_of(levels[i]).start()
        if at == AUX_AT:
            exchange_aux()
        if groups == 1:
            ours = [turns[i][0] for i in both if not turns[i][1]]
            if ours:
                combine(*ours)

    if groups > 1:
        for i in range(npairs - 1, 0, -2):
            combine(i, i - 1)

    rim = auxg.at[:, 0]

    @pl.when(has_down)
    def _():
        pltpu.make_async_copy(rim, rim, ah_rs.at[0]).wait()

    @pl.when(has_up)
    def _():
        pltpu.make_async_copy(rim, rim, ah_rs.at[1]).wait()

    place = block * urows - HALO + lax.broadcasted_iota(jnp.int32, (erows, LANES), 0)
    inside = (place >= 0) & (place < nlat * rows)
    lane = lax.broadcasted_iota(jnp.int32, (erows, LANES), 1)
    tiles = LANES // cols
    for q in range(flon // LANES):
        first, second = (
            auxg[tiles * q + i].astype(F32).reshape(erows, 2 * LANES) for i in range(2)
        )
        lhs = jnp.concatenate([first[:, :LANES], second[:, :LANES]], axis=1)
        upper = jnp.floor(lhs * (1.0 / 256.0))
        lower = lhs - 256.0 * upper
        out = dot(jnp.concatenate([upper.astype(BF16), lower.astype(BF16)], axis=0), spread[...])
        out = 256.0 * out[:erows] + out[erows:]
        at = slice(q * LANES, (q + 1) * LANES)
        for t in range(STEPS):
            weight = out[:, t * LANES : (t + 1) * LANES]
            value = out[:, (STEPS + t) * LANES : (STEPS + t + 1) * LANES]
            cell = out[:, (2 * STEPS + t) * LANES : (2 * STEPS + t + 1) * LANES]
            hit = cell == CELL * (lane % OBLK).astype(F32)
            wts[t, :, at] = jnp.where(hit, weight * (WEIGHT_MAX / CODES), 0.0)
            vals[t, :, at] = value * (VALUE_MAX / CODES)
        w0, w1 = (w[:, LANES:] * (WIND_MAX / CODES) for w in (first, second))
        left = lane < cols
        c0 = jnp.where(left, w0, pltpu.roll(w1, cols, 1))
        c1 = jnp.where(left, pltpu.roll(w0, cols, 1), w1)
        east_in = inside & (lane + q * LANES < flon - 1)
        west_in = inside & (lane + q * LANES > 0)
        coef[0, :, at] = jnp.where(inside, DIFFUSION - 0.5 * c1, 0.0)
        coef[1, :, at] = jnp.where(inside, DIFFUSION + 0.5 * c1, 0.0)
        coef[2, :, at] = jnp.where(east_in, DIFFUSION - 0.5 * c0, 0.0)
        coef[3, :, at] = jnp.where(west_in, DIFFUSION + 0.5 * c0, 0.0)
        coef[4, :, at] = jnp.where(inside, jnp.full((erows, LANES), 1.0 - 4.0 * DIFFUSION, F32), 0.0)

    await_bytes((npairs - 1) * unit_bytes, rs_rs.at[0])
    total = pr[pair]
    for i in range(1, npairs):
        p = pair ^ i
        total = total + decode(rs[p], rs_step[p]).reshape(urows, flon)
    total = total * scale
    ext[HALO : HALO + urows] = total

    def rim_total(side):
        await_bytes(npairs * edge_bytes, halo_rs.at[side])
        return sum(decode(hq[side, p], hq_step[side, p]) for p in range(npairs)) * scale

    @pl.when(has_up)
    def _():
        ext[:HALO] = rim_total(0)

    @pl.when(has_down)
    def _():
        ext[HALO + urows :] = rim_total(1)

    state = ext[...]
    for t in range(STEPS):
        state = (
            coef[4] * state
            + coef[0] * pltpu.roll(state, erows - 1, 0)
            + coef[1] * pltpu.roll(state, 1, 0)
            + coef[2] * pltpu.roll(state, flon - 1, 1)
            + coef[3] * pltpu.roll(state, 1, 1)
        )
        wts[t] = wts[t] * (state - vals[t])
    adjoint = None
    for t in reversed(range(STEPS)):
        adjoint = wts[t] if adjoint is None else adjoint + wts[t]
        adjoint = (
            coef[4] * adjoint
            + pltpu.roll(coef[1] * adjoint, erows - 1, 0)
            + pltpu.roll(coef[0] * adjoint, 1, 0)
            + pltpu.roll(coef[3] * adjoint, flon - 1, 1)
            + pltpu.roll(coef[2] * adjoint, 1, 1)
        )
    adjq[me], adj_step[me] = encode(
        adjoint[HALO : HALO + urows].reshape(urows // SUB, SUB, flon)
    )

    def unit_copies(unit, ss, rsem, mem):
        return (
            send(adjq.at[unit], adjq.at[unit], ss, rsem, mem, z),
            send(adj_step.at[unit], adj_step.at[unit], ss, rsem, mem, z),
        )

    def share_adjoint(i):
        for copy in unit_copies(me, gone, adj_rs.at[pair], held(i)[0]):
            copy.start()

    for i in range(1, npairs):
        share_adjoint(i)

    def relay(i):
        for copy in unit_copies(held(i)[0], gone, rel_rs.at[pair ^ i], partner):
            copy.start()

    def inc_copy(there):
        return send(
            itile.at[there],
            incr.at[my_level, pl.ds(pl.multiple_of(my_row, 8), urows)],
            inc_out,
            inc_rs.at[0],
            there,
            z,
        )

    def inc_all(sem):
        these = itile.at[pl.ds(0, nmem - 1)]
        return pltpu.make_async_copy(these, these, sem)

    def share_increment():
        for m in range(nmem):
            itile[m] = ext[HALO : HALO + urows, m * cols : (m + 1) * cols]
        for i in range(1, nmem):
            inc_copy((me + i) % nmem).start()
        incr[my_level, pl.ds(pl.multiple_of(my_row, 8), urows)] = itile[me]

    direct = lev if nlat <= REACH + 1 else 0
    reach = REACH if direct else 2

    def g_copies(way, step, k, batch, straight):
        there = z + step * k
        js = pl.ds(batch[0], len(batch))
        src = gq.at[there, js], gq_step.at[there, js]
        if k > 2 and not straight:
            lat, arrived = z + step, relayed_rs.at[way, k - 3, batch[0]]
            dst = relayed.at[way, k - 3, js], relayed_step.at[way, k - 3, js]
        else:
            slot = reach * way + k - 1
            lat, arrived = there, g_rs.at[slot]
            dst = gr.at[slot, js], gr_step.at[slot, js]
        return [send(a, b, gone, arrived, me, lat) for a, b in zip(src, dst)]

    def g_start(batch, straight, distances):
        for k in distances:
            for way, step in directions:
                ready = exists(z + step * k)
                if k > 1 and not straight:
                    ready = ready & jnp.logical_not(exists(z - step))

                @pl.when(ready)
                def _():
                    for copy in g_copies(way, step, k, batch, straight):
                        copy.start()

    def g_later(batch):
        for k in range(nlat - 2, 1, -1):
            for way, step in directions:
                there = z + step * k

                @pl.when(exists(there) & exists(z - step))
                def _():
                    arrived = relayed_rs.at[way, k - 2, batch[0]]
                    await_bytes(len(batch) * band_bytes, arrived)
                    for j in batch:
                        more = decode(relayed[way, k - 2, j], relayed_step[way, k - 2, j])
                        codes, unit = encode((gb[there, j] + more)[None])
                        gq[there, j], gq_step[there, j] = codes[0], unit
                    for copy in g_copies(way, step, k, batch, False):
                        copy.start()

    def backward(j, level):
        field = jnp.concatenate(
            [
                decode(adjq[level * groups + g], adj_step[level * groups + g]).reshape(urows, flon)
                for g in range(groups)
            ],
            axis=0,
        )
        product = jnp.concatenate(
            [pert_ref[m, level].astype(F32) * field for m in range(members)], axis=0
        )
        hi, lo = split2(product)
        projected = dot(jnp.concatenate([hi, lo], axis=1), lon_t[...])
        projected = jnp.concatenate(
            [projected[m * rows : (m + 1) * rows] for m in range(members)], axis=1
        )
        hi, lo = split2(projected)
        banded = dot(lat_t2, jnp.concatenate([hi, lo], axis=0)).reshape(nlat, cband, width)
        gb[:, j] = banded
        for b in range(nlat):
            codes, unit = encode(banded[b : b + 1])
            gq[b, j], gq_step[b, j] = codes[0], unit

    def take(i):
        if i:
            await_bytes(unit_bytes, adj_rs.at[pair ^ i])
        relay(i)

    def taken(i):
        await_bytes(unit_bytes, rel_rs.at[pair ^ i])

    batches = [(j, j + 1) for j in range(0, lev, 2)]
    if groups == 1:
        batches = [(j,) for j in range(lev)]

    def later(batch):
        if batch[0] < lev - direct:
            g_later(batch)

    def nearest(batch):
        g_start(batch, True, (1,))

    for b, batch in enumerate(batches):
        if groups == 2:
            for j in batch:
                take(j)
            for j in batch:
                taken(j)
        else:
            if b == 0:
                take(0)
            if b == 2:
                for i in range(1, npairs - 1):
                    take(i)
            if batch[0] == npairs:
                take(npairs - 1)
            for j in batch:
                if not turns_back[j][1]:
                    taken(turns_back[j][0])
        for j in batch:
            backward(j, levels_back[j])
        g_start(batch, batch[0] >= lev - direct, range(nlat - 1, 1, -1))
        if b < 2:
            nearest(batch)
        if b == 2:
            share_increment()
        if b > 2:
            nearest(batches[b - 1])
        if b > 1:
            later(batches[b - 2])
    nearest(batches[-1])
    for batch in batches[-2:]:
        later(batch)

    inc_all(inc_rs.at[0]).wait()
    inc_ref[...] = incr[...].reshape(lev * rows, cols)

    for k in range(1, reach + 1):
        for way, step in directions:
            slot = reach * way + k - 1
            first = 0 if k < 3 else lev - direct

            @pl.when(exists(z - step * k))
            def _():
                await_bytes((lev - first) * band_bytes, g_rs.at[slot])
                for j in range(first, lev):
                    gb[z, j] = gb[z, j] + decode(gr[slot, j], gr_step[slot, j])

    for j in range(lev):
        gsum[levels_back[j]] = gb[z, j]
    for m in range(members):
        total = jnp.swapaxes(gsum[:, :, m * clon : (m + 1) * clon], 0, 1)
        total = total * scale
        for c in range(total.shape[0]):
            at = (c * members + m) * lev
            grad_ref[at : at + lev] = total[c] + coarse_ref[c, m].astype(F32)

    await_bytes(all_bytes, gone)
    inc_all(inc_out).wait()
    rim_bytes = rim.size * 2 + npairs * edge_bytes

    @pl.when(has_up)
    def _():
        await_bytes(rim_bytes, in_sem.at[1])

    @pl.when(has_down)
    def _():
        await_bytes(rim_bytes, in_sem.at[2])


def finish_kernel(banded_ref, tiles_ref, grad_ref, inc_ref):
    grad_ref[...] = banded_ref[...]
    inc_ref[...] = tiles_ref[...]


def body(
    nmem,
    nlat,
    coarse_weights,
    perturbations,
    lat_matrix,
    lon_matrix,
    wind_field,
    observed_cell,
    observed_value,
    observed_weight,
):
    members, lev, rows, flon = perturbations.shape
    cband, _, _, clon = coarse_weights.shape
    cols = wind_field.shape[2]
    blocks = cols // OBLK
    groups = nmem // lev
    urows = rows // groups
    erows = urows + 2 * HALO
    npairs = nmem // 2
    assert nmem == lev * groups and nmem % 2 == 0 and groups <= 2 and urows % 8 == 0 and urows >= HALO
    assert 2 * cols == LANES and 3 * STEPS * blocks <= LANES
    assert npairs & (npairs - 1) == 0 and HALO == SUB and cband == SUB
    vmem = pl.BlockSpec(memory_space=pltpu.VMEM)
    dma = pltpu.SemaphoreType.DMA
    width = members * clon
    chunks = urows // SUB
    hops = nlat - 3 if nlat > REACH + 1 else 1
    unit_bytes = urows * flon * 2 + ROW
    band_bytes = cband * width * 2 + ROW
    all_bytes = (
        (nlat - 1) * coarse_weights.size * 2
        + (nmem - 1) * urows * 2 * LANES * 2
        + npairs * urows * flon * 4
        + (3 * npairs - 2) * unit_bytes
        + (nlat - 1) * lev * band_bytes
    )
    arguments = (
        coarse_weights,
        perturbations,
        lat_matrix,
        lon_matrix,
        wind_field,
        jnp.swapaxes(observed_cell, 2, 3),
        jnp.swapaxes(observed_value, 2, 3),
        jnp.swapaxes(observed_weight, 2, 3),
    )
    banded, increment = pl.pallas_call(
        functools.partial(
            kernel, nmem, nlat, float(1.0 / (members * nmem - 1) ** 0.5), all_bytes
        ),
        out_shape=(
            pltpu.VMEM((cband * members * lev, clon), F32),
            pltpu.VMEM((lev * rows, cols), F32),
        ),
        in_specs=[pl.BlockSpec(memory_space=pltpu.HBM)] * len(arguments),
        out_specs=(vmem, vmem),
        scratch_shapes=[
            *[pltpu.VMEM(x.shape, x.dtype) for x in arguments],
            pltpu.VMEM((lev, rows // SUB, SUB, 2 * LANES), I16),
            pltpu.VMEM((nlat, lev, members, cband, clon), BF16),
            pltpu.VMEM((nmem, erows // SUB, SUB, 2 * LANES), I16),
            pltpu.VMEM((nmem, urows, flon), F32),
            pltpu.VMEM((npairs, urows, flon), F32),
            pltpu.VMEM((npairs, chunks, SUB, flon), I16),
            pltpu.VMEM((npairs, 1, LANES), F32),
            pltpu.VMEM((npairs, chunks, SUB, flon), I16),
            pltpu.VMEM((npairs, 1, LANES), F32),
            pltpu.VMEM((2, npairs, SUB, flon), I16),
            pltpu.VMEM((2, npairs, 1, LANES), F32),
            pltpu.VMEM((erows, flon), F32),
            pltpu.VMEM((2 * LANES, 3 * STEPS * LANES), BF16),
            pltpu.VMEM((5, erows, flon), F32),
            pltpu.VMEM((STEPS, erows, flon), F32),
            pltpu.VMEM((STEPS, erows, flon), F32),
            pltpu.VMEM((nmem, urows, cols), F32),
            pltpu.VMEM((lev, rows, cols), F32),
            pltpu.VMEM((nmem, chunks, SUB, flon), I16),
            pltpu.VMEM((nmem, 1, LANES), F32),
            pltpu.VMEM((nlat, lev, cband, width), F32),
            pltpu.VMEM((nlat, lev, cband, width), I16),
            pltpu.VMEM((nlat, lev, 1, LANES), F32),
            pltpu.VMEM((6, lev, cband, width), I16),
            pltpu.VMEM((6, lev, 1, LANES), F32),
            pltpu.VMEM((2, hops, lev if nlat > REACH + 1 else 1, cband, width), I16),
            pltpu.VMEM((2, hops, lev if nlat > REACH + 1 else 1, 1, LANES), F32),
            pltpu.VMEM((2 * flon, clon), BF16),
            pltpu.VMEM((2 * clon, flon), BF16),
            pltpu.VMEM((all_bytes // ROW, 1, LANES), F32),
            pltpu.VMEM((lev, cband, width), F32),
            dma((len(arguments),)),
            dma((lev,)),
            dma((1,)),
            dma((2,)),
            dma((npairs,)),
            dma((1,)),
            dma((2,)),
            dma((1,)),
            dma((npairs,)),
            dma((npairs,)),
            dma((6,)),
            dma((2, hops, lev if nlat > REACH + 1 else 1)),
        ],
        compiler_params=pltpu.CompilerParams(
            collective_id=0, has_side_effects=True, vmem_limit_bytes=40 * 1024 * 1024
        ),
    )(*[pltpu.with_memory_space_constraint(x, pltpu.HBM) for x in arguments])
    gradient, increment = pl.pallas_call(
        finish_kernel,
        out_shape=(
            jax.ShapeDtypeStruct((cband * members * lev, clon), F32),
            jax.ShapeDtypeStruct((lev * rows, cols), F32),
        ),
        in_specs=[vmem] * 2,
        out_specs=(vmem, vmem),
        compiler_params=pltpu.CompilerParams(vmem_limit_bytes=4 * 1024 * 1024),
    )(banded, increment)
    return gradient.reshape(coarse_weights.shape), increment.reshape(lev, rows, cols)


def solution(mesh):
    in_specs = (
        P("lat", "mem", None, None),
        P("mem", None, "lat", None),
        P("lat", None),
        P(),
        P(None, "lat", "mem"),
        P(None, None, "lat", "mem"),
        P(None, None, "lat", "mem"),
        P(None, None, "lat", "mem"),
    )
    out_specs = (P("lat", "mem", None, None), P(None, "lat", "mem"))
    call = functools.partial(body, mesh.shape["mem"], mesh.shape["lat"])
    return jax.shard_map(call, mesh=mesh, in_specs=in_specs, out_specs=out_specs, check_vma=False)
```

```python
import functools

import jax
import jax.numpy as jnp
from jax import lax
from jax.experimental import pallas as pl
from jax.experimental.pallas import tpu as pltpu
from jax.sharding import PartitionSpec as P

STEPS = 4
OBLK = 8
HALO = 2 * STEPS
SUB = 8
AUX_AT = 2
REACH = 3
LANES = 128
ROW = 4 * LANES
DIFFUSION = 0.2
CODES = 32767.0
WEIGHT_MAX = 4.0
VALUE_MAX = 6.0
WIND_MAX = 0.4
CELL = 4096.0
TINY = 1e-30
F32 = jnp.float32
BF16 = jnp.bfloat16
I16 = jnp.int16


def split2(x):
    hi = x.astype(BF16)
    return hi, (x - hi.astype(F32)).astype(BF16)


def dot(a, b, dims=((1,), (0,))):
    return lax.dot_general(a, b, (dims, ((), ())), preferred_element_type=F32)


def spans(width):
    return [slice(at, at + LANES) for at in range(0, width, LANES)]


def encode(x):
    size = jnp.abs(x)
    peak = functools.reduce(jnp.maximum, [size[i] for i in range(x.shape[0])])
    peak = functools.reduce(jnp.maximum, [peak[:, at] for at in spans(x.shape[2])])
    step = jnp.maximum(jnp.max(peak, axis=0, keepdims=True), TINY) * (1.0 / CODES)
    inverse = 1.0 / step
    scaled = jnp.concatenate([x[:, :, at] * inverse for at in spans(x.shape[2])], axis=2)
    return jnp.round(scaled).astype(jnp.int32).astype(I16), step


def decode(codes, step):
    values = codes.astype(F32)
    return jnp.concatenate([values[..., at] * step for at in spans(codes.shape[-1])], axis=-1)


def kernel(
    nmem,
    nlat,
    scale,
    all_bytes,
    coarse_hbm,
    pert_hbm,
    lat_hbm,
    lon_hbm,
    wind_hbm,
    cell_hbm,
    value_hbm,
    weight_hbm,
    grad_ref,
    inc_ref,
    coarse_ref,
    pert_ref,
    lat_ref,
    lon_ref,
    wind_ref,
    cell_ref,
    value_ref,
    weight_ref,
    aux_ref,
    cg,
    auxg,
    part,
    pr,
    rq,
    rq_step,
    rs,
    rs_step,
    hq,
    hq_step,
    ext,
    spread,
    coef,
    wts,
    vals,
    itile,
    incr,
    adjq,
    adj_step,
    gb,
    gq,
    gq_step,
    gr,
    gr_step,
    relayed,
    relayed_step,
    lon_t,
    lon_2,
    amount,
    gsum,
    in_sem,
    cg_rs,
    aux_rs,
    ah_rs,
    pr_rs,
    rs_rs,
    halo_rs,
    inc_rs,
    adj_rs,
    rel_rs,
    g_rs,
    relayed_rs,
):
    members, lev, rows, flon = pert_ref.shape
    clon = lon_ref.shape[0]
    cband, width = gb.shape[2:]
    cols = flon // nmem
    groups = nmem // lev
    urows = rows // groups
    erows = urows + 2 * HALO
    npairs = nmem // 2
    chunks = urows // SUB
    me = lax.axis_index("mem")
    z = lax.axis_index("lat")
    pair = me // 2
    core = me % 2
    partner = pair * 2 + (1 - core)
    my_level = me // groups
    my_group = me % groups
    my_row = my_group * urows
    block = z * groups + my_group
    has_up = block > 0
    has_down = block < nlat * groups - 1
    unit_bytes = urows * flon * 2 + ROW
    edge_bytes = HALO * flon * 2 + ROW
    band_bytes = cband * width * 2 + ROW

    def neighbour(unit, shift):
        there = block + shift
        home = (unit // groups) * groups
        return home + (there + groups) % groups, (there + groups) // groups - 1

    up = neighbour(me, -1)
    down = neighbour(me, 1)

    def send(src, dst, ss, rsem, mem, lat):
        return pltpu.make_async_remote_copy(
            src_ref=src,
            dst_ref=dst,
            send_sem=ss,
            recv_sem=rsem,
            device_id={"mem": mem, "lat": lat},
            device_id_type=pl.DeviceIdType.MESH,
        )

    def await_bytes(count, sem):
        these = amount.at[pl.ds(0, count // ROW)]
        pltpu.make_async_copy(these, these, sem).wait()

    arguments = (
        (coarse_hbm, coarse_ref),
        (lat_hbm, lat_ref),
        (lon_hbm, lon_ref),
        (wind_hbm, wind_ref),
        (cell_hbm, cell_ref),
        (value_hbm, value_ref),
        (weight_hbm, weight_ref),
        (pert_hbm, pert_ref),
    )
    loads = [
        pltpu.make_async_copy(src, dst, in_sem.at[i]) for i, (src, dst) in enumerate(arguments)
    ]
    for load in loads:
        load.start()

    gone, inc_out = in_sem.at[0], in_sem.at[3]
    barrier = pltpu.get_barrier_semaphore()

    def greet(mem, lat):
        pl.semaphore_signal(
            barrier, inc=1, device_id={"mem": mem, "lat": lat}, device_id_type=pl.DeviceIdType.MESH
        )

    for i in range(1, nlat):
        greet(me, (z + i) % nlat)
    for i in range(1, nmem):
        greet((me + i) % nmem, z)
    far_up = has_up & (my_group == 0)
    far_down = has_down & (my_group == groups - 1)
    others = range(1, npairs) if groups == 1 else range(npairs)

    def held(i):
        mine = core if i == 0 or groups == 2 else 1 - core
        return 2 * (pair ^ i) + mine, 2 * (pair ^ i) + 1 - mine


    @pl.when(far_up)
    def _():
        for i in others:
            greet(*neighbour(held(i)[0], -1))

    @pl.when(far_down)
    def _():
        for i in others:
            greet(*neighbour(held(i)[0], 1))

    def position(level):
        if groups > 1:
            return level
        away = pair ^ (level // 2)
        mine = jnp.where(away == 0, core, 1 - core) == level % 2
        theirs = jnp.maximum(0, 2 * (npairs - 1 - away) - 1)
        return jnp.where(mine, jnp.minimum(lev - 1, 2 * (npairs - away)), theirs)

    loads[0].wait()
    for m in range(members):
        mine = jnp.swapaxes(coarse_ref[:, m].astype(F32), 0, 1).astype(BF16)
        for level in range(lev):
            cg[z, position(level), m] = mine[level]
    more = jnp.where(far_up, len(others), 0) + jnp.where(far_down, len(others), 0)
    pl.semaphore_wait(barrier, nmem + nlat - 2 + more)

    if groups == 1:
        turns = [(npairs - 1, True)]
        for i in range(npairs - 1, 0, -1):
            turns += [(i - 1, True), (i, False)]
        turns += [(0, False)]
        levels = [held(i)[1 if theirs else 0] for i, theirs in turns]
        turns_back = [(0, True), (0, False)]
        for mine in (True, False):
            turns_back += [(i, mine) for i in range(1, npairs - 1)]
        turns_back += [(npairs - 1, True), (npairs - 1, False)]
        levels_back = [held(i)[0 if mine else 1] for i, mine in turns_back]
    else:
        levels = list(range(lev))
        turns_back = [(i, True) for i in range(npairs)]
        levels_back = [pair ^ i for i in range(npairs)]

    def exists(place):
        return (place >= 0) & (place < nlat)

    directions = ((0, 1), (1, -1))

    def start(a, distances):
        for k in distances:
            for _, step in directions:
                there = z + step * k

                @pl.when(exists(there))
                def _():
                    these = cg.at[z, pl.ds(sets[a][0], len(sets[a]))]
                    send(these, these, gone, cg_rs.at[a], me, there).start()

    sets = [(i, i + 1) for i in range(0, lev, 2)]
    if groups == 1:
        sets = [(i,) for i in range(lev)]
    last = len(sets) - 1
    at_end = (z == 0) | (z == nlat - 1)

    @pl.when(at_end)
    def _():
        for a in range(last + 1):
            start(a, range(nlat - 1, 1, -1))
            if a:
                start(a - 1, (1,))
        start(last, (1,))

    @pl.when(jnp.logical_not(at_end))
    def _():
        for a in range(last + 1):
            start(a, range(nlat - 1, 0, -1))

    def await_coarse(a):
        these = cg.at[pl.ds(0, nlat - 1), pl.ds(sets[a][0], len(sets[a]))]
        pltpu.make_async_copy(these, these, cg_rs.at[a]).wait()

    for load in loads[1:-1]:
        load.wait()

    blank = jnp.zeros((LANES - 3 * STEPS * (cols // OBLK), rows), F32)
    spot = lax.broadcasted_iota(jnp.int32, (rows, LANES), 1) // (STEPS * (cols // OBLK))
    units = jnp.where(spot == 0, CODES / WEIGHT_MAX, jnp.where(spot == 1, CODES / VALUE_MAX, CELL))

    def coded(x):
        return jnp.round(x).astype(jnp.int32).astype(I16).reshape(rows // SUB, SUB, LANES)

    winds = coded(jnp.concatenate([wind_ref[0], wind_ref[1]], axis=1) * (CODES / WIND_MAX))

    def pack(level, carry):
        pieces = [ref[t, level] for ref in (weight_ref, value_ref) for t in range(STEPS)]
        pieces += [cell_ref[t, level].astype(F32) for t in range(STEPS)]
        seen = jnp.transpose(jnp.concatenate(pieces + [blank], axis=0)) * units
        aux_ref[level, :, :, :LANES] = coded(seen)
        aux_ref[level, :, :, LANES:] = winds
        return carry

    lax.fori_loop(0, lev, pack, 0)

    def aux_copy(there):
        return send(
            aux_ref.at[there // groups, pl.ds((there % groups) * chunks, chunks)],
            auxg.at[me, pl.ds(1, chunks)],
            gone,
            aux_rs.at[0],
            there,
            z,
        )

    def aux_all(sem):
        these = auxg.at[pl.ds(0, nmem - 1), pl.ds(1, chunks)]
        return pltpu.make_async_copy(these, these, sem.at[0])

    for i in range(1, nmem):
        aux_copy((me + i) % nmem).start()

    auxg[me, 1 : 1 + chunks] = aux_ref[my_level, pl.ds(my_group * chunks, chunks)]

    @pl.when(jnp.logical_not(has_up))
    def _():
        auxg[:, :1] = jnp.zeros((nmem, 1, SUB, 2 * LANES), I16)
        ext[:HALO] = jnp.zeros((HALO, flon), F32)

    @pl.when(jnp.logical_not(has_down))
    def _():
        auxg[:, 1 + chunks :] = jnp.zeros((nmem, 1, SUB, 2 * LANES), I16)
        ext[HALO + urows :] = jnp.zeros((HALO, flon), F32)

    per_tile = cols // OBLK
    k = lax.broadcasted_iota(jnp.int32, (2 * LANES, LANES), 0)
    n = lax.broadcasted_iota(jnp.int32, (2 * LANES, LANES), 1)
    for piece in range(3 * STEPS):
        hit = k == (n // cols) * LANES + piece * per_tile + (n % cols) // OBLK
        spread[:, piece * LANES : (piece + 1) * LANES] = jnp.where(hit, 1.0, 0.0).astype(BF16)

    lat_f32 = lat_ref[...].astype(F32)
    lat_bf = lat_ref[...]
    lat_t = jnp.transpose(lat_f32).astype(BF16)
    lat_t2 = jnp.concatenate([lat_t, lat_t], axis=1)
    lon = lon_ref[...]
    lon_t[:flon] = jnp.transpose(lon.astype(F32)).astype(BF16)
    lon_t[flon:] = lon_t[:flon]
    lon_2[:clon] = lon
    lon_2[clon:] = lon

    loads[-1].wait()

    def pr_copy(i):
        p = pair ^ i
        return send(part.at[held(i)[1]], pr.at[p], gone, pr_rs.at[p], partner, z)

    def pr_copy_of(p):
        return send(part.at[2 * p + 1 - core], pr.at[p], gone, pr_rs.at[p], partner, z)

    def rs_copies(i):
        unit = held(i)[0]
        return (
            send(rq.at[pair ^ i], rs.at[pair], gone, rs_rs.at[0], unit, z),
            send(rq_step.at[pair ^ i], rs_step.at[pair], gone, rs_rs.at[0], unit, z),
        )

    def halo_copies(i, side):
        mem, lat = neighbour(held(i)[0], 1 if side == 0 else -1)
        rim = chunks - 1 if side == 0 else 0
        sems = in_sem.at[2 - side], halo_rs.at[side]
        return (
            send(rq.at[pair ^ i, rim], hq.at[side, pair], *sems, mem, lat),
            send(rq_step.at[pair ^ i], hq_step.at[side, pair], *sems, mem, lat),
        )

    def combine(*places):
        for i in places:
            pr_copy(i).wait_recv()
        for i in places:
            p = pair ^ i
            whole = pr[p] + part[held(i)[0]]
            pr[p] = whole
            rq[p], rq_step[p] = encode(whole.reshape(chunks, SUB, flon))
        for i in places:
            if i:
                for copy in rs_copies(i):
                    copy.start()

        @pl.when(has_down)
        def _():
            for i in places:
                for copy in halo_copies(i, 0):
                    copy.start()

        @pl.when(has_up)
        def _():
            for i in places:
                for copy in halo_copies(i, 1):
                    copy.start()

    ah_up = send(
        auxg.at[:, 1], auxg.at[:, 1 + chunks], in_sem.at[1], ah_rs.at[0], *up
    )
    ah_down = send(auxg.at[:, chunks], auxg.at[:, 0], in_sem.at[2], ah_rs.at[1], *down)

    def exchange_aux():
        aux_all(aux_rs).wait()

        @pl.when(has_up)
        def _():
            ah_up.start()

        @pl.when(has_down)
        def _():
            ah_down.start()

    def forward(i, level):
        coarse = jnp.concatenate(
            [cg[:, i, m].astype(F32).reshape(-1, clon) for m in range(members)], axis=1
        ).astype(BF16)
        partly = dot(lat_bf, coarse)
        partly = jnp.concatenate(
            [partly[:, m * clon : (m + 1) * clon] for m in range(members)], axis=0
        )
        localized = dot(jnp.concatenate(split2(partly), axis=1), lon_2[...])
        total = localized[:rows] * pert_ref[0, level].astype(F32)
        for m in range(1, members):
            total += localized[m * rows : (m + 1) * rows] * pert_ref[m, level].astype(F32)
        part[pl.ds(level * groups, groups)] = total.reshape(groups, urows, flon)

    for at, both in enumerate(sets):
        await_coarse(at)
        for i in both:
            forward(i, levels[i])
        if groups == 1:
            for i in both:
                if turns[i][1]:
                    pr_copy(turns[i][0]).start()
        else:
            for i in both:
                pr_copy_of(levels[i]).start()
        if at == AUX_AT:
            exchange_aux()
        if groups == 1:
            ours = [turns[i][0] for i in both if not turns[i][1]]
            if ours:
                combine(*ours)

    if groups > 1:
        for i in range(npairs - 1, 0, -2):
            combine(i, i - 1)

    rim = auxg.at[:, 0]

    @pl.when(has_down)
    def _():
        pltpu.make_async_copy(rim, rim, ah_rs.at[0]).wait()

    @pl.when(has_up)
    def _():
        pltpu.make_async_copy(rim, rim, ah_rs.at[1]).wait()

    place = block * urows - HALO + lax.broadcasted_iota(jnp.int32, (erows, LANES), 0)
    inside = (place >= 0) & (place < nlat * rows)
    lane = lax.broadcasted_iota(jnp.int32, (erows, LANES), 1)
    tiles = LANES // cols
    for q in range(flon // LANES):
        first, second = (
            auxg[tiles * q + i].astype(F32).reshape(erows, 2 * LANES) for i in range(2)
        )
        lhs = jnp.concatenate([first[:, :LANES], second[:, :LANES]], axis=1)
        upper = jnp.floor(lhs * (1.0 / 256.0))
        lower = lhs - 256.0 * upper
        out = dot(jnp.concatenate([upper.astype(BF16), lower.astype(BF16)], axis=0), spread[...])
        out = 256.0 * out[:erows] + out[erows:]
        at = slice(q * LANES, (q + 1) * LANES)
        for t in range(STEPS):
            weight = out[:, t * LANES : (t + 1) * LANES]
            value = out[:, (STEPS + t) * LANES : (STEPS + t + 1) * LANES]
            cell = out[:, (2 * STEPS + t) * LANES : (2 * STEPS + t + 1) * LANES]
            hit = cell == CELL * (lane % OBLK).astype(F32)
            wts[t, :, at] = jnp.where(hit, weight * (WEIGHT_MAX / CODES), 0.0)
            vals[t, :, at] = value * (VALUE_MAX / CODES)
        w0, w1 = (w[:, LANES:] * (WIND_MAX / CODES) for w in (first, second))
        left = lane < cols
        c0 = jnp.where(left, w0, pltpu.roll(w1, cols, 1))
        c1 = jnp.where(left, pltpu.roll(w0, cols, 1), w1)
        east_in = inside & (lane + q * LANES < flon - 1)
        west_in = inside & (lane + q * LANES > 0)
        coef[0, :, at] = jnp.where(inside, DIFFUSION - 0.5 * c1, 0.0)
        coef[1, :, at] = jnp.where(inside, DIFFUSION + 0.5 * c1, 0.0)
        coef[2, :, at] = jnp.where(east_in, DIFFUSION - 0.5 * c0, 0.0)
        coef[3, :, at] = jnp.where(west_in, DIFFUSION + 0.5 * c0, 0.0)
        coef[4, :, at] = jnp.where(inside, jnp.full((erows, LANES), 1.0 - 4.0 * DIFFUSION, F32), 0.0)

    await_bytes((npairs - 1) * unit_bytes, rs_rs.at[0])
    total = pr[pair]
    for i in range(1, npairs):
        p = pair ^ i
        total = total + decode(rs[p], rs_step[p]).reshape(urows, flon)
    total = total * scale
    ext[HALO : HALO + urows] = total

    def rim_total(side):
        await_bytes(npairs * edge_bytes, halo_rs.at[side])
        return sum(decode(hq[side, p], hq_step[side, p]) for p in range(npairs)) * scale

    @pl.when(has_up)
    def _():
        ext[:HALO] = rim_total(0)

    @pl.when(has_down)
    def _():
        ext[HALO + urows :] = rim_total(1)

    state = ext[...]
    for t in range(STEPS):
        state = (
            coef[4] * state
            + coef[0] * pltpu.roll(state, erows - 1, 0)
            + coef[1] * pltpu.roll(state, 1, 0)
            + coef[2] * pltpu.roll(state, flon - 1, 1)
            + coef[3] * pltpu.roll(state, 1, 1)
        )
        wts[t] = wts[t] * (state - vals[t])
    adjoint = None
    for t in reversed(range(STEPS)):
        adjoint = wts[t] if adjoint is None else adjoint + wts[t]
        adjoint = (
            coef[4] * adjoint
            + pltpu.roll(coef[1] * adjoint, erows - 1, 0)
            + pltpu.roll(coef[0] * adjoint, 1, 0)
            + pltpu.roll(coef[3] * adjoint, flon - 1, 1)
            + pltpu.roll(coef[2] * adjoint, 1, 1)
        )
    adjq[me], adj_step[me] = encode(
        adjoint[HALO : HALO + urows].reshape(urows // SUB, SUB, flon)
    )

    def unit_copies(unit, ss, rsem, mem):
        return (
            send(adjq.at[unit], adjq.at[unit], ss, rsem, mem, z),
            send(adj_step.at[unit], adj_step.at[unit], ss, rsem, mem, z),
        )

    def share_adjoint(i):
        for copy in unit_copies(me, gone, adj_rs.at[pair], held(i)[0]):
            copy.start()

    for i in range(1, npairs):
        share_adjoint(i)

    def relay(i):
        for copy in unit_copies(held(i)[0], gone, rel_rs.at[pair ^ i], partner):
            copy.start()

    def inc_copy(there):
        return send(
            itile.at[there],
            incr.at[my_level, pl.ds(pl.multiple_of(my_row, 8), urows)],
            inc_out,
            inc_rs.at[0],
            there,
            z,
        )

    def inc_all(sem):
        these = itile.at[pl.ds(0, nmem - 1)]
        return pltpu.make_async_copy(these, these, sem)

    def share_increment():
        for m in range(nmem):
            itile[m] = ext[HALO : HALO + urows, m * cols : (m + 1) * cols]
        for i in range(1, nmem):
            inc_copy((me + i) % nmem).start()
        incr[my_level, pl.ds(pl.multiple_of(my_row, 8), urows)] = itile[me]

    direct = lev if nlat <= REACH + 1 else 0
    reach = REACH if direct else 2

    def g_copies(way, step, k, batch, straight):
        there = z + step * k
        js = pl.ds(batch[0], len(batch))
        src = gq.at[there, js], gq_step.at[there, js]
        if k > 2 and not straight:
            lat, arrived = z + step, relayed_rs.at[way, k - 3, batch[0]]
            dst = relayed.at[way, k - 3, js], relayed_step.at[way, k - 3, js]
        else:
            slot = reach * way + k - 1
            lat, arrived = there, g_rs.at[slot]
            dst = gr.at[slot, js], gr_step.at[slot, js]
        return [send(a, b, gone, arrived, me, lat) for a, b in zip(src, dst)]

    def g_start(batch, straight, distances):
        for k in distances:
            for way, step in directions:
                ready = exists(z + step * k)
                if k > 1 and not straight:
                    ready = ready & jnp.logical_not(exists(z - step))

                @pl.when(ready)
                def _():
                    for copy in g_copies(way, step, k, batch, straight):
                        copy.start()

    def g_later(batch):
        for k in range(nlat - 2, 1, -1):
            for way, step in directions:
                there = z + step * k

                @pl.when(exists(there) & exists(z - step))
                def _():
                    arrived = relayed_rs.at[way, k - 2, batch[0]]
                    await_bytes(len(batch) * band_bytes, arrived)
                    for j in batch:
                        more = decode(relayed[way, k - 2, j], relayed_step[way, k - 2, j])
                        codes, unit = encode((gb[there, j] + more)[None])
                        gq[there, j], gq_step[there, j] = codes[0], unit
                    for copy in g_copies(way, step, k, batch, False):
                        copy.start()

    def backward(j, level):
        field = jnp.concatenate(
            [
                decode(adjq[level * groups + g], adj_step[level * groups + g]).reshape(urows, flon)
                for g in range(groups)
            ],
            axis=0,
        )
        product = jnp.concatenate(
            [pert_ref[m, level].astype(F32) * field for m in range(members)], axis=0
        )
        hi, lo = split2(product)
        projected = dot(jnp.concatenate([hi, lo], axis=1), lon_t[...])
        projected = jnp.concatenate(
            [projected[m * rows : (m + 1) * rows] for m in range(members)], axis=1
        )
        hi, lo = split2(projected)
        banded = dot(lat_t2, jnp.concatenate([hi, lo], axis=0)).reshape(nlat, cband, width)
        gb[:, j] = banded
        for b in range(nlat):
            codes, unit = encode(banded[b : b + 1])
            gq[b, j], gq_step[b, j] = codes[0], unit

    def take(i):
        if i:
            await_bytes(unit_bytes, adj_rs.at[pair ^ i])
        relay(i)

    def taken(i):
        await_bytes(unit_bytes, rel_rs.at[pair ^ i])

    batches = [(j, j + 1) for j in range(0, lev, 2)]
    if groups == 1:
        batches = [(j,) for j in range(lev)]

    def later(batch):
        if batch[0] < lev - direct:
            g_later(batch)

    def nearest(batch):
        g_start(batch, True, (1,))

    for b, batch in enumerate(batches):
        if groups == 2:
            for j in batch:
                take(j)
            for j in batch:
                taken(j)
        else:
            if b == 0:
                take(0)
            if b == 2:
                for i in range(1, npairs - 1):
                    take(i)
            if batch[0] == npairs:
                take(npairs - 1)
            for j in batch:
                if not turns_back[j][1]:
                    taken(turns_back[j][0])
        for j in batch:
            backward(j, levels_back[j])
        g_start(batch, batch[0] >= lev - direct, range(nlat - 1, 1, -1))
        if b < 2:
            nearest(batch)
        if b == 2:
            share_increment()
        if b > 3:
            nearest(batches[b - 2])
        if b > 1:
            later(batches[b - 2])
    nearest(batches[-2])
    nearest(batches[-1])
    for batch in batches[-2:]:
        later(batch)

    inc_all(inc_rs.at[0]).wait()
    inc_ref[...] = incr[...].reshape(lev * rows, cols)

    for k in range(1, reach + 1):
        for way, step in directions:
            slot = reach * way + k - 1
            first = 0 if k < 3 else lev - direct

            @pl.when(exists(z - step * k))
            def _():
                await_bytes((lev - first) * band_bytes, g_rs.at[slot])
                for j in range(first, lev):
                    gb[z, j] = gb[z, j] + decode(gr[slot, j], gr_step[slot, j])

    for j in range(lev):
        gsum[levels_back[j]] = gb[z, j]
    for m in range(members):
        total = jnp.swapaxes(gsum[:, :, m * clon : (m + 1) * clon], 0, 1)
        total = total * scale
        for c in range(total.shape[0]):
            at = (c * members + m) * lev
            grad_ref[at : at + lev] = total[c] + coarse_ref[c, m].astype(F32)

    await_bytes(all_bytes, gone)
    inc_all(inc_out).wait()
    rim_bytes = rim.size * 2 + npairs * edge_bytes

    @pl.when(has_up)
    def _():
        await_bytes(rim_bytes, in_sem.at[1])

    @pl.when(has_down)
    def _():
        await_bytes(rim_bytes, in_sem.at[2])


def finish_kernel(banded_ref, tiles_ref, grad_ref, inc_ref):
    grad_ref[...] = banded_ref[...]
    inc_ref[...] = tiles_ref[...]


def body(
    nmem,
    nlat,
    coarse_weights,
    perturbations,
    lat_matrix,
    lon_matrix,
    wind_field,
    observed_cell,
    observed_value,
    observed_weight,
):
    members, lev, rows, flon = perturbations.shape
    cband, _, _, clon = coarse_weights.shape
    cols = wind_field.shape[2]
    blocks = cols // OBLK
    groups = nmem // lev
    urows = rows // groups
    erows = urows + 2 * HALO
    npairs = nmem // 2
    assert nmem == lev * groups and nmem % 2 == 0 and groups <= 2 and urows % 8 == 0 and urows >= HALO
    assert 2 * cols == LANES and 3 * STEPS * blocks <= LANES
    assert npairs & (npairs - 1) == 0 and HALO == SUB and cband == SUB
    vmem = pl.BlockSpec(memory_space=pltpu.VMEM)
    dma = pltpu.SemaphoreType.DMA
    width = members * clon
    chunks = urows // SUB
    hops = nlat - 3 if nlat > REACH + 1 else 1
    unit_bytes = urows * flon * 2 + ROW
    band_bytes = cband * width * 2 + ROW
    all_bytes = (
        (nlat - 1) * coarse_weights.size * 2
        + (nmem - 1) * urows * 2 * LANES * 2
        + npairs * urows * flon * 4
        + (3 * npairs - 2) * unit_bytes
        + (nlat - 1) * lev * band_bytes
    )
    arguments = (
        coarse_weights,
        perturbations,
        lat_matrix,
        lon_matrix,
        wind_field,
        jnp.swapaxes(observed_cell, 2, 3),
        jnp.swapaxes(observed_value, 2, 3),
        jnp.swapaxes(observed_weight, 2, 3),
    )
    banded, increment = pl.pallas_call(
        functools.partial(
            kernel, nmem, nlat, float(1.0 / (members * nmem - 1) ** 0.5), all_bytes
        ),
        out_shape=(
            pltpu.VMEM((cband * members * lev, clon), F32),
            pltpu.VMEM((lev * rows, cols), F32),
        ),
        in_specs=[pl.BlockSpec(memory_space=pltpu.HBM)] * len(arguments),
        out_specs=(vmem, vmem),
        scratch_shapes=[
            *[pltpu.VMEM(x.shape, x.dtype) for x in arguments],
            pltpu.VMEM((lev, rows // SUB, SUB, 2 * LANES), I16),
            pltpu.VMEM((nlat, lev, members, cband, clon), BF16),
            pltpu.VMEM((nmem, erows // SUB, SUB, 2 * LANES), I16),
            pltpu.VMEM((nmem, urows, flon), F32),
            pltpu.VMEM((npairs, urows, flon), F32),
            pltpu.VMEM((npairs, chunks, SUB, flon), I16),
            pltpu.VMEM((npairs, 1, LANES), F32),
            pltpu.VMEM((npairs, chunks, SUB, flon), I16),
            pltpu.VMEM((npairs, 1, LANES), F32),
            pltpu.VMEM((2, npairs, SUB, flon), I16),
            pltpu.VMEM((2, npairs, 1, LANES), F32),
            pltpu.VMEM((erows, flon), F32),
            pltpu.VMEM((2 * LANES, 3 * STEPS * LANES), BF16),
            pltpu.VMEM((5, erows, flon), F32),
            pltpu.VMEM((STEPS, erows, flon), F32),
            pltpu.VMEM((STEPS, erows, flon), F32),
            pltpu.VMEM((nmem, urows, cols), F32),
            pltpu.VMEM((lev, rows, cols), F32),
            pltpu.VMEM((nmem, chunks, SUB, flon), I16),
            pltpu.VMEM((nmem, 1, LANES), F32),
            pltpu.VMEM((nlat, lev, cband, width), F32),
            pltpu.VMEM((nlat, lev, cband, width), I16),
            pltpu.VMEM((nlat, lev, 1, LANES), F32),
            pltpu.VMEM((6, lev, cband, width), I16),
            pltpu.VMEM((6, lev, 1, LANES), F32),
            pltpu.VMEM((2, hops, lev if nlat > REACH + 1 else 1, cband, width), I16),
            pltpu.VMEM((2, hops, lev if nlat > REACH + 1 else 1, 1, LANES), F32),
            pltpu.VMEM((2 * flon, clon), BF16),
            pltpu.VMEM((2 * clon, flon), BF16),
            pltpu.VMEM((all_bytes // ROW, 1, LANES), F32),
            pltpu.VMEM((lev, cband, width), F32),
            dma((len(arguments),)),
            dma((lev,)),
            dma((1,)),
            dma((2,)),
            dma((npairs,)),
            dma((1,)),
            dma((2,)),
            dma((1,)),
            dma((npairs,)),
            dma((npairs,)),
            dma((6,)),
            dma((2, hops, lev if nlat > REACH + 1 else 1)),
        ],
        compiler_params=pltpu.CompilerParams(
            collective_id=0, has_side_effects=True, vmem_limit_bytes=40 * 1024 * 1024
        ),
    )(*[pltpu.with_memory_space_constraint(x, pltpu.HBM) for x in arguments])
    gradient, increment = pl.pallas_call(
        finish_kernel,
        out_shape=(
            jax.ShapeDtypeStruct((cband * members * lev, clon), F32),
            jax.ShapeDtypeStruct((lev * rows, cols), F32),
        ),
        in_specs=[vmem] * 2,
        out_specs=(vmem, vmem),
        compiler_params=pltpu.CompilerParams(vmem_limit_bytes=4 * 1024 * 1024),
    )(banded, increment)
    return gradient.reshape(coarse_weights.shape), increment.reshape(lev, rows, cols)


def solution(mesh):
    in_specs = (
        P("lat", "mem", None, None),
        P("mem", None, "lat", None),
        P("lat", None),
        P(),
        P(None, "lat", "mem"),
        P(None, None, "lat", "mem"),
        P(None, None, "lat", "mem"),
        P(None, None, "lat", "mem"),
    )
    out_specs = (P("lat", "mem", None, None), P(None, "lat", "mem"))
    call = functools.partial(body, mesh.shape["mem"], mesh.shape["lat"])
    return jax.shard_map(call, mesh=mesh, in_specs=in_specs, out_specs=out_specs, check_vma=False)
```
